32 devices in a mesh: dp: 8 (over y, x, core), mp: 4 (over z).
Axes of the slice: x: 2, y: 2, z: 4, core: 2. Of those that a mesh axis runs over, the one named last changes fastest.
Arguments:
- tokens: bfloat16 [8192, 2048], P(('dp', 'mp')), may hold values from -6 to 6
- cotangent: bfloat16 [8192, 2048], P(('dp', 'mp')), may hold values from -6 to 6
- lengths: int32 [8], P('dp'), may hold values from 256 to 1024, as said below
- query_weight: bfloat16 [2048, 2048], P(None, 'mp'), may hold values from -0.1875 to 0.1875
- key_weight: bfloat16 [2048, 2048], P(None, 'mp'), may hold values from -0.1875 to 0.1875
- value_weight: bfloat16 [2048, 2048], P(None, 'mp'), may hold values from -0.125 to 0.125
- out_weight: bfloat16 [2048, 2048], P('mp'), may hold values from -2 to 2
- gate_weight: bfloat16 [2048, 8192], P(None, 'mp'), may hold values from -0.125 to 0.125
- up_weight: bfloat16 [2048, 8192], P(None, 'mp'), may hold values from -0.125 to 0.125
- down_weight: bfloat16 [8192, 2048], P('mp'), may hold values from -0.0625 to 0.0625
- attn_gain: float32 [2048], replicated, may hold values from 0.5 to 1.5
- mlp_gain: float32 [2048], replicated, may hold values from 0.5 to 1.5
- memory_gate: float32 [16], P('mp'), may hold values from -2 to 2
Outputs:
- block_out: bfloat16 [8192, 2048], P(('dp', 'mp'))
- grad_tokens: float32 [8192, 2048], P(('dp', 'mp'))
- grad_query: float32 [2048, 2048], P('dp', 'mp')
- grad_key: float32 [2048, 2048], P('dp', 'mp')
- grad_value: float32 [2048, 2048], P('dp', 'mp')
- grad_out: float32 [2048, 2048], P('mp', 'dp')
- grad_gate: float32 [2048, 8192], P('dp', 'mp')
- grad_up: float32 [2048, 8192], P('dp', 'mp')
- grad_down: float32 [8192, 2048], P('mp', 'dp')
- grad_attn_gain: float32 [2048], replicated
- grad_mlp_gain: float32 [2048], replicated
- grad_memory_gate: float32 [16], replicated
The draws below stay inside these ranges and needn't reach their ends.
Inputs may be any that keep to these rules, and one draw needn't show every extreme that they name: `lengths`: some group holds a sequence of exactly 1024 rows in every draw.
All inputs are finite; a program needn't handle non-finite values.
Results may differ from the reference program's by a relative error of at most 0.013.
The reference program's roundings to bfloat16 on the way count: a program that leaves them out, or rounds other values in their place, can miss the bound.
Values may be sent and summed in bfloat16 or wider, within the bound.
No kernel may reach another device: no remote copies, remote signals or barrier semaphores. Data moves between devices by JAX's collectives and lax.ppermute only.
A program may use at most 320 MiB of HBM per device.

```python
import jax
import jax.numpy as jnp
from jax import lax

D = 2048
FF = 8192
DK = 128
H = 16
SEG = 128
TOK = 1024
NSEG = 8
LEN_MIN = 256
TOKENS = 8192
N_DP = 8


def draw_lengths(key, part):
    key_draw = jax.random.fold_in(key, 11)
    key_pick = jax.random.fold_in(key, 23)
    drawn = jax.random.randint(key_draw, (N_DP,), LEN_MIN, TOK + 1)
    chosen = jax.random.randint(key_pick, (), 0, N_DP)
    return jnp.where(jnp.arange(N_DP) == chosen, TOK, drawn).astype(jnp.int32)


def block_scale(stream_key, extent, split, low, high):
    gain = 1.0
    for dim, blocks in split:
        heights = jax.random.uniform(jax.random.fold_in(jax.random.fold_in(stream_key, 6), dim), (blocks,), jnp.float32, low / len(split), high / len(split))
        gain = gain * jnp.repeat(jnp.exp(heights), extent[dim] // blocks).reshape((-1,) + (1,) * (len(extent) - 1 - dim))
    return gain


def scatter_about(key, extent, deviation, bound, split=(), kind=jnp.bfloat16):
    values = jax.random.normal(key, extent, jnp.float32) * deviation
    if len(split) > 0:
        values = block_scale(key, extent, split, -0.22, 0.18) * values
    return jnp.clip(values, min=-bound, max=bound).astype(kind)


def setup_inputs(seed: int = 0) -> dict:
    key_list = jax.random.split(jax.random.key(seed), 14)
    tokens = scatter_about(key_list[0], (TOKENS, D), 1.0, 6.0, ((0, 32),))
    cotangent = scatter_about(key_list[1], (TOKENS, D), 1.0, 6.0, ((0, 32),))
    lengths = draw_lengths(jax.random.fold_in(key_list[13], 71), 0)
    query_weight = scatter_about(key_list[3], (D, D), (D // 2) ** -0.5, 0.1875, ((1, 4),))
    key_weight = scatter_about(key_list[4], (D, D), (D // 2) ** -0.5, 0.1875, ((1, 4),))
    value_weight = scatter_about(key_list[5], (D, D), D ** -0.5, 0.125, ((1, 4),))
    out_weight = scatter_about(key_list[6], (D, D), (max(D // 256, 1)) ** -0.5, 2.0, ((0, 4),))
    gate_weight = scatter_about(key_list[7], (D, FF), D ** -0.5, 0.125, ((1, 4),))
    up_weight = scatter_about(key_list[8], (D, FF), D ** -0.5, 0.125, ((1, 4),))
    down_weight = scatter_about(key_list[9], (FF, D), FF ** -0.5, 0.0625, ((0, 4),))
    attn_gain = jnp.clip(1.0 + 0.1 * jax.random.normal(key_list[10], (D,), jnp.float32), 0.5, 1.5)
    mlp_gain = jnp.clip(1.0 + 0.1 * jax.random.normal(key_list[11], (D,), jnp.float32), 0.5, 1.5)
    memory_gate = jnp.clip(jax.random.uniform(key_list[12], (H,), jnp.float32, -2.0, 2.0) * block_scale(key_list[12], (H,), ((0, 4),), -0.4, 0.0), -2.0, 2.0)
    return {"tokens": tokens, "cotangent": cotangent, "lengths": lengths, "query_weight": query_weight, "key_weight": key_weight, "value_weight": value_weight, "out_weight": out_weight, "gate_weight": gate_weight, "up_weight": up_weight, "down_weight": down_weight, "attn_gain": attn_gain, "mlp_gain": mlp_gain, "memory_gate": memory_gate}


EPS = 1e-05
HIGHEST = lax.Precision.HIGHEST

@jax.custom_vjp
def low(v):
    return lax.optimization_barrier(v.astype(jnp.bfloat16)).astype(jnp.float32)

@jax.custom_vjp
def low_back(v):
    return v

def low_keep(v):
    return (low(v), None)

def low_pass(kept, grad):
    return (grad,)

def back_keep(v):
    return (v, None)

def back_low(kept, grad):
    return (low(grad),)
low.defvjp(low_keep, low_pass)
low_back.defvjp(back_keep, back_low)

def normed(values, gain_vec):
    return values * lax.rsqrt(lax.optimization_barrier(jnp.mean(values * values, axis=-1, keepdims=True)) + EPS) * gain_vec

def lifted(values):
    return jnp.where(values > 0, values + 1.0, jnp.exp(jnp.minimum(values, 0.0)))

def segment_step(carried, block_in, mix_gate):
    memory, normer = carried
    queries, key_rows, value_rows, live_rows = block_in
    lifted_q = lifted(queries)
    lifted_k = lifted(key_rows)
    recalled = jnp.einsum('shd,hde->she', lifted_q, memory, precision=HIGHEST)
    recalled = recalled / jnp.einsum('shd,hd->sh', lifted_q, normer, precision=HIGHEST)[:, :, None]
    scores = low_back(jnp.einsum('qhd,khd->hqk', queries, key_rows, precision=HIGHEST) * DK ** (-0.5))
    causal = jnp.arange(SEG)[:, None] >= jnp.arange(SEG)[None, :]
    scores = jnp.where(causal[None], scores, -1e+30)
    weights = low(jax.nn.softmax(scores, axis=-1))
    in_block = low_back(jnp.einsum('hqk,khd->qhd', weights, value_rows, precision=HIGHEST))
    mixed = mix_gate * recalled + (1.0 - mix_gate) * in_block
    guessed = jnp.einsum('shd,hde->she', lifted_k, memory, precision=HIGHEST)
    guessed = guessed / jnp.einsum('shd,hd->sh', lifted_k, normer, precision=HIGHEST)[:, :, None]
    written = lifted_k * live_rows[:, None, None]
    memory = memory + jnp.einsum('shd,she->hde', written, value_rows - guessed, precision=HIGHEST)
    normer = normer + lax.optimization_barrier(jnp.sum(written, axis=0))
    return ((memory, normer), mixed)

def layer(inputs, live, query_weight, key_weight, value_weight, out_weight, gate_weight, up_weight, down_weight, attn_gain, mlp_gain, memory_gate):
    head_count = query_weight.shape[1] // DK
    normed_one = low(normed(inputs, attn_gain))

    def project(weight_cols):
        return low_back(low(jnp.dot(normed_one, weight_cols, precision=HIGHEST))).reshape(NSEG, SEG, head_count, DK)
    queries = project(query_weight)
    key_rows = project(key_weight)
    value_rows = project(value_weight)
    mix_gate = jax.nn.sigmoid(memory_gate)[None, :, None]

    def stepper(carried, block_in):
        return segment_step(carried, block_in, mix_gate)
    start_state = (jnp.zeros((head_count, DK, DK), jnp.float32), jnp.ones((head_count, DK), jnp.float32))
    _, mixed = lax.scan(jax.checkpoint(stepper), start_state, (queries, key_rows, value_rows, live.reshape(NSEG, SEG)))
    mixed = low(mixed.reshape(TOK, head_count * DK))
    state = inputs + low_back(live[:, None] * jnp.dot(mixed, out_weight, precision=HIGHEST))
    normed_two = low(normed(state, mlp_gain))
    gate_pre = low_back(jnp.dot(normed_two, gate_weight, precision=HIGHEST))
    up_pre = low_back(jnp.dot(normed_two, up_weight, precision=HIGHEST))
    hidden = low(jax.nn.gelu(gate_pre) * up_pre)
    return state + low_back(live[:, None] * jnp.dot(hidden, down_weight, precision=HIGHEST))

def reference(tokens, cotangent, lengths, query_weight, key_weight, value_weight, out_weight, gate_weight, up_weight, down_weight, attn_gain, mlp_gain, memory_gate):
    matrices = (query_weight, key_weight, value_weight, out_weight, gate_weight, up_weight, down_weight)
    params = tuple((matrix.astype(jnp.float32) for matrix in matrices)) + (attn_gain, mlp_gain, memory_gate)
    inputs = tokens.astype(jnp.float32).reshape(N_DP, TOK, D)
    upstream = cotangent.astype(jnp.float32).reshape(N_DP, TOK, D)

    def one_group(summed, item):
        group_in, group_up, length = item
        live = (jnp.arange(TOK) < length).astype(jnp.float32)

        def forward(group_rows, *weight_list):
            return layer(group_rows, live, *weight_list)
        result, pull = jax.vjp(forward, group_in, *params)
        grads = pull(group_up)
        summed = tuple((acc + part for acc, part in zip(summed, grads[1:])))
        return (summed, (result, grads[0]))
    zeros_init = tuple((jnp.zeros_like(param) for param in params))
    summed, (results, grad_inputs) = lax.scan(one_group, zeros_init, (inputs, upstream, lengths))
    return (results.reshape(TOKENS, D).astype(jnp.bfloat16), grad_inputs.reshape(TOKENS, D), summed[0], summed[1], summed[2], summed[3], summed[4], summed[5], summed[6], summed[7], summed[8], summed[9])
```

```python
import functools

import jax
import jax.numpy as jnp
from jax import lax
from jax.experimental import pallas as pl
from jax.experimental.pallas import tpu as pltpu
from jax.sharding import PartitionSpec as P

DK = 128
SEG = 128
EPS = 1e-05
NEGATIVE = -1e30
LOW = jnp.bfloat16
F32 = jnp.float32


def hop(value, axis, mask):
    size = lax.axis_size(axis)
    return lax.ppermute(value, axis, [(j, j ^ mask) for j in range(size)])


def top_bit(number):
    return 1 << (number.bit_length() - 1)


def singles(size):
    return [p for p in range(1, size) if p == top_bit(p)]


def doubles(size):
    return [p for p in range(1, size) if p != top_bit(p)]


def gather_near(mine, axis):
    return {0: mine, **{p: hop(mine, axis, p) for p in singles(lax.axis_size(axis))}}


def gather_far(pieces, axis):
    size = lax.axis_size(axis)
    return {p: hop(pieces[top_bit(p)], axis, p ^ top_bit(p)) for p in doubles(size)}


def reduce_far(parts, axis):
    size = lax.axis_size(axis)
    return {p: hop(parts[p].astype(LOW), axis, p ^ top_bit(p)) for p in doubles(size)}


def reduce_near(parts, got, axis, only=None):
    size = lax.axis_size(axis)
    sent = {}
    for p in singles(size):
        if only is None or p in only:
            value = parts[p].astype(F32)
            for q in doubles(size):
                if top_bit(q) == p:
                    value = value + got[q].astype(F32)
            sent[p] = hop(value.astype(LOW), axis, p)
    return sent


def total(own, *arrived):
    value = own.astype(F32)
    for some in arrived:
        for p in some:
            value = value + some[p].astype(F32)
    return value


def swap_pieces(pieces, axis):
    return {p: hop(pieces[p], axis, p) if p else pieces[p] for p in range(lax.axis_size(axis))}


def stacked(pieces, axis=0):
    return jnp.concatenate([pieces[p] for p in range(len(pieces))], axis=axis)


def relative_blocks(value, axis):
    size = lax.axis_size(axis)
    mine = lax.axis_index(axis)
    step = value.shape[1] // size

    def take(r):
        return lax.dynamic_slice_in_dim(value, (mine ^ r) * step, step, axis=1)

    return (
        jnp.concatenate([take(r) for r in range(0, size, 2)], axis=1),
        jnp.concatenate([take(r) for r in range(1, size, 2)], axis=1),
    )


class BlockSum:
    def __init__(self, kept, sent, axis, dim):
        self.axis, self.dim, self.kept = axis, dim, kept
        self.size = lax.axis_size(axis)
        self.masks = [1 << b for b in range(1, self.size.bit_length() - 1)]
        self.flight = hop(sent, axis, 1)
        self.halves = None

    def part(self, value, j, low):
        step = self.kept.shape[self.dim] // (self.size // 2)
        if self.dim == 0:
            half = step // 2
            return value[j * step + low * half : j * step + (low + 1) * half].astype(F32)
        half = self.kept.shape[0] // 2
        return value[low * half : (low + 1) * half, j * step : (j + 1) * step].astype(F32)

    def step(self, k):
        if k == 0:
            self.halves = [
                {
                    2 * j: self.part(self.kept, j, low) + self.part(self.flight, j, low)
                    for j in range(self.size // 2)
                }
                for low in (0, 1)
            ]
        else:
            self.land(k - 1)
        self.flight = []
        for low, order in ((0, self.masks), (1, self.masks[::-1])):
            held = self.halves[low]
            gone = [r for r in held if r & order[k]]
            self.flight.append(
                hop(jnp.stack([held[r] for r in gone]).astype(LOW), self.axis, order[k])
            )

    def land(self, k):
        for low, order in ((0, self.masks), (1, self.masks[::-1])):
            held = self.halves[low]
            gone = [r for r in held if r & order[k]]
            self.halves[low] = {
                r ^ order[k]: held[r ^ order[k]] + self.flight[low][n].astype(F32)
                for n, r in enumerate(gone)
            }

    @property
    def steps(self):
        return len(self.masks)

    def result(self):
        self.land(self.steps - 1)
        return jnp.concatenate([half[0] for half in self.halves], axis=0)

    @property
    def state(self):
        return self.kept, self.flight, self.halves

    @state.setter
    def state(self, value):
        self.kept, self.flight, self.halves = value


def sum_everywhere(vector, axes):
    for axis in axes:
        bit = 1
        while bit < lax.axis_size(axis):
            vector = vector + hop(vector, axis, bit)
            bit *= 2
    return vector


def rows_by(left, right, contract, precision=None):
    return lax.dot_general(
        left, right, ((contract[:1], contract[1:]), ((), ())), preferred_element_type=F32
    )


def split(value):
    high = value.astype(LOW)
    return high, (value - high.astype(F32)).astype(LOW)


def fine(left, right, contract):
    (lh, ll), (rh, rl) = split(left), split(right)
    return (
        rows_by(lh, rh, contract) + rows_by(lh, rl, contract) + rows_by(ll, rh, contract)
    )


def lifted(values):
    return jnp.where(values > 0, values + 1.0, jnp.exp(jnp.minimum(values, 0.0)))


def lifted_slope(values):
    slope = jnp.exp(jnp.minimum(values, 0.0))
    return jnp.where(values > 0, 1.0, jnp.where(values < 0, slope, 0.5))


def probabilities(queries, key_rows):
    scores = rows_by(queries, key_rows, (1, 1)) * DK ** (-0.5)
    row = lax.broadcasted_iota(jnp.int32, (SEG, SEG), 0)
    col = lax.broadcasted_iota(jnp.int32, (SEG, SEG), 1)
    scores = jnp.where(row >= col, scores, NEGATIVE)
    lift = jnp.exp(scores - jnp.max(scores, axis=-1, keepdims=True))
    return lift / jnp.sum(lift, axis=-1, keepdims=True)


def live_column(segment, length):
    position = segment * SEG + lax.broadcasted_iota(jnp.int32, (SEG, 1), 0)
    return (position < length).astype(F32)


def attend_kernel(place, share, qkv_ref, mixed_ref, memory_ref, normer_ref, memory, normer):
    heads = memory.shape[0]
    width = heads * DK
    segment = pl.program_id(0)

    @pl.when(segment == 0)
    def _():
        memory[...] = jnp.zeros_like(memory)
        normer[...] = jnp.ones_like(normer)

    live = live_column(segment, place[1])
    memory_ref[0] = memory[...]
    normer_ref[0] = normer[...]
    for h in range(heads):
        at = h * DK
        queries = qkv_ref[:, at : at + DK]
        key_rows = qkv_ref[:, width + at : width + at + DK]
        value_rows = qkv_ref[:, 2 * width + at : 2 * width + at + DK]
        probs = probabilities(queries, key_rows).astype(LOW)
        in_block = rows_by(probs, value_rows, (1, 0))
        lifted_q = lifted(queries.astype(F32))
        lifted_k = lifted(key_rows.astype(F32))
        held = memory[h]
        norm = normer[h : h + 1]
        read = fine(jnp.concatenate([lifted_q, lifted_k], axis=0), held, (1, 0))
        recalled = read[:SEG] / jnp.sum(lifted_q * norm, axis=-1, keepdims=True)
        guessed = read[SEG:] / jnp.sum(lifted_k * norm, axis=-1, keepdims=True)
        mix = share[h]
        mixed_ref[:, at : at + DK] = (mix * recalled + (1.0 - mix) * in_block).astype(LOW)
        written = lifted_k * live
        memory[h] = held + fine(written, value_rows.astype(F32) - guessed, (0, 0))
        normer[h : h + 1] = norm + jnp.sum(written, axis=0, keepdims=True)


def attend_back_kernel(
    place, share, qkv_ref, grad_ref, memory_ref, normer_ref, out_ref, mix_ref, grad_memory, grad_normer
):
    heads = grad_memory.shape[0]
    width = heads * DK
    step = pl.program_id(0)
    segment = pl.num_programs(0) - 1 - step

    @pl.when(step == 0)
    def _():
        grad_memory[...] = jnp.zeros_like(grad_memory)
        grad_normer[...] = jnp.zeros_like(grad_normer)
        mix_ref[...] = jnp.zeros_like(mix_ref)

    live = live_column(segment, place[1])
    for h in range(heads):
        at = h * DK
        queries = qkv_ref[:, at : at + DK]
        key_rows = qkv_ref[:, width + at : width + at + DK]
        value_rows = qkv_ref[:, 2 * width + at : 2 * width + at + DK]
        grad_mixed = grad_ref[:, at : at + DK].astype(F32)
        mix = share[h]
        probs = probabilities(queries, key_rows)
        probs_low = probs.astype(LOW)
        in_block = rows_by(probs_low, value_rows, (1, 0))
        grad_local = ((1.0 - mix) * grad_mixed).astype(LOW)
        back_v = rows_by(probs_low, grad_local, (0, 0))
        grad_probs = rows_by(grad_local, value_rows, (1, 1))
        inner = jnp.sum(grad_probs * probs, axis=-1, keepdims=True)
        grad_scores = (probs * (grad_probs - inner)).astype(LOW)
        back_q = rows_by(grad_scores, key_rows, (1, 0)) * DK ** (-0.5)
        back_k = rows_by(grad_scores, queries, (0, 0)) * DK ** (-0.5)
        float_q = queries.astype(F32)
        float_k = key_rows.astype(F32)
        lifted_q = lifted(float_q)
        lifted_k = lifted(float_k)
        both = jnp.concatenate([lifted_q, lifted_k], axis=0)
        held = memory_ref[0, h]
        norm = normer_ref[0, h : h + 1]
        over_q = 1.0 / jnp.sum(lifted_q * norm, axis=-1, keepdims=True)
        over_k = 1.0 / jnp.sum(lifted_k * norm, axis=-1, keepdims=True)
        read = fine(both, held, (1, 0))
        recalled = read[:SEG] * over_q
        guessed = read[SEG:] * over_k
        mix_ref[h : h + 1] += jnp.sum(
            grad_mixed * (recalled - in_block), axis=0, keepdims=True
        )
        grad_held = grad_memory[h]
        grad_norm = grad_normer[h : h + 1]
        written = lifted_k * live
        grad_update = fine(written, grad_held, (1, 0))
        grad_written = fine(value_rows.astype(F32) - guessed, grad_held, (1, 1)) + grad_norm
        grad_recalled = mix * grad_mixed
        grad_read_q = grad_recalled * over_q
        grad_read_k = -grad_update * over_k
        grad_sum_q = -jnp.sum(grad_read_q * recalled, axis=-1, keepdims=True)
        grad_sum_k = -jnp.sum(grad_read_k * guessed, axis=-1, keepdims=True)
        grad_reads = jnp.concatenate([grad_read_q, grad_read_k], axis=0)
        back = fine(grad_reads, held, (1, 1))
        grad_lifted_q = back[:SEG] + grad_sum_q * norm
        grad_lifted_k = back[SEG:] + grad_sum_k * norm + live * grad_written
        grad_memory[h] = grad_held + fine(both, grad_reads, (0, 0))
        grad_normer[h : h + 1] = grad_norm + jnp.sum(
            lifted_q * grad_sum_q + lifted_k * grad_sum_k, axis=0, keepdims=True
        )
        out_ref[:, at : at + DK] = (back_q + grad_lifted_q * lifted_slope(float_q)).astype(LOW)
        out_ref[:, width + at : width + at + DK] = (
            back_k + grad_lifted_k * lifted_slope(float_k)
        ).astype(LOW)
        out_ref[:, 2 * width + at : 2 * width + at + DK] = (back_v + grad_update).astype(LOW)


def segment_place(segment, place, per_chunk):
    chunk = lax.div(segment, per_chunk) ^ place[0]
    return chunk * per_chunk + lax.rem(segment, per_chunk)


def attend(qkv, place, share, per_chunk):
    rows, wide = qkv.shape
    heads = wide // (3 * DK)
    blocks = rows // SEG

    def row_map(step, place):
        return (segment_place(step, place, per_chunk), 0)

    return pl.pallas_call(
        attend_kernel,
        name="attend",
        out_shape=(
            jax.ShapeDtypeStruct((rows, heads * DK), LOW),
            jax.ShapeDtypeStruct((blocks, heads, DK, DK), F32),
            jax.ShapeDtypeStruct((blocks, heads, DK), F32),
        ),
        grid_spec=pltpu.PrefetchScalarGridSpec(
            num_scalar_prefetch=1,
            grid=(blocks,),
            in_specs=[
                pl.BlockSpec(memory_space=pltpu.SMEM),
                pl.BlockSpec((SEG, wide), row_map),
            ],
            out_specs=[
                pl.BlockSpec((SEG, heads * DK), row_map),
                pl.BlockSpec((1, heads, DK, DK), lambda step, place: (step, 0, 0, 0)),
                pl.BlockSpec((1, heads, DK), lambda step, place: (step, 0, 0)),
            ],
            scratch_shapes=[pltpu.VMEM((heads, DK, DK), F32), pltpu.VMEM((heads, DK), F32)],
        ),
        compiler_params=pltpu.CompilerParams(
            dimension_semantics=("arbitrary",), vmem_limit_bytes=24 << 20
        ),
        cost_estimate=pl.CostEstimate(
            flops=blocks * heads * 14 * 2 * SEG**3 * 4,
            bytes_accessed=rows * wide * 4,
            transcendentals=0,
        ),
    )(place, share, qkv)


def attend_back(qkv, grad_mixed, memories, normers, place, share, per_chunk):
    rows, wide = qkv.shape
    heads = wide // (3 * DK)
    blocks = rows // SEG

    def row_map(step, place):
        return (segment_place(blocks - 1 - step, place, per_chunk), 0)

    return pl.pallas_call(
        attend_back_kernel,
        name="attend_back",
        out_shape=(
            jax.ShapeDtypeStruct((rows, wide), LOW),
            jax.ShapeDtypeStruct((heads, DK), F32),
        ),
        grid_spec=pltpu.PrefetchScalarGridSpec(
            num_scalar_prefetch=1,
            grid=(blocks,),
            in_specs=[
                pl.BlockSpec(memory_space=pltpu.SMEM),
                pl.BlockSpec((SEG, wide), row_map),
                pl.BlockSpec((SEG, heads * DK), row_map),
                pl.BlockSpec(
                    (1, heads, DK, DK), lambda step, place: (blocks - 1 - step, 0, 0, 0)
                ),
                pl.BlockSpec((1, heads, DK), lambda step, place: (blocks - 1 - step, 0, 0)),
            ],
            out_specs=[
                pl.BlockSpec((SEG, wide), row_map),
                pl.BlockSpec((heads, DK), lambda step, place: (0, 0)),
            ],
            scratch_shapes=[pltpu.VMEM((heads, DK, DK), F32), pltpu.VMEM((heads, DK), F32)],
        ),
        compiler_params=pltpu.CompilerParams(
            dimension_semantics=("arbitrary",), vmem_limit_bytes=24 << 20
        ),
        cost_estimate=pl.CostEstimate(
            flops=blocks * heads * 30 * 2 * SEG**3 * 4,
            bytes_accessed=rows * wide * 6,
            transcendentals=0,
        ),
    )(place, share, qkv, grad_mixed, memories, normers)


def live_rows(place, rows):
    position = place[0] * rows + lax.broadcasted_iota(jnp.int32, (rows, 1), 0)
    return (position < place[1]).astype(F32)


def out_project_kernel(place, *refs):
    *mixed_refs, out_ref, tokens_ref, gain_ref, state_ref, normed_ref = refs
    step = pl.program_id(0)

    @pl.when(step == 0)
    def _():
        state_ref[...] = jnp.zeros_like(state_ref)

    weight = out_ref[...].reshape(-1, out_ref.shape[-1])
    for k, mixed_ref in enumerate(mixed_refs):

        @pl.when(step == k)
        def _():
            state_ref[...] += rows_by(mixed_ref[...], weight, (1, 0))

    @pl.when(step == len(mixed_refs) - 1)
    def _():
        live = live_rows(place, state_ref.shape[0])
        state = tokens_ref[...].astype(F32) + live * state_ref[...]
        state_ref[...] = state
        normed_ref[...] = (state * inverse_rms(state) * gain_ref[...]).astype(LOW)


def out_spec(out_full):
    blocks, _, rows, features = out_full.shape
    return pl.BlockSpec((blocks, 1, rows, features), lambda step, *_: (0, step, 0, 0))


def whole(shape):
    return pl.BlockSpec(shape, lambda *_: (0,) * len(shape))


def out_project(mixed, out_full, tokens, gain, place):
    ranks = len(mixed)
    rows, features = tokens.shape
    width = mixed[0].shape[1]
    return pl.pallas_call(
        out_project_kernel,
        name="out_project",
        out_shape=(
            jax.ShapeDtypeStruct((rows, features), F32),
            jax.ShapeDtypeStruct((rows, features), LOW),
        ),
        grid_spec=pltpu.PrefetchScalarGridSpec(
            num_scalar_prefetch=1,
            grid=(ranks,),
            in_specs=[whole((rows, width))] * ranks
            + [out_spec(out_full), whole((rows, features)), whole((1, features))],
            out_specs=[whole((rows, features))] * 2,
        ),
        compiler_params=pltpu.CompilerParams(
            dimension_semantics=("arbitrary",), vmem_limit_bytes=24 << 20
        ),
        cost_estimate=pl.CostEstimate(
            flops=2 * rows * features * ranks * width,
            bytes_accessed=2 * ranks * width * features,
            transcendentals=0,
        ),
    )(place, *[mixed[p] for p in range(ranks)], out_full, tokens, gain[None])


def out_back_kernel(grad_ref, out_ref, back_ref):
    weight = out_ref[...].reshape(-1, out_ref.shape[-1])
    back_ref[0] = rows_by(grad_ref[...], weight, (1, 1)).astype(LOW)


def out_back(grad_attn, out_full):
    rows, features = grad_attn.shape
    blocks, ranks, slice_rows, _ = out_full.shape
    width = blocks * slice_rows
    return pl.pallas_call(
        out_back_kernel,
        name="out_back",
        out_shape=jax.ShapeDtypeStruct((ranks, rows, width), LOW),
        grid=(ranks,),
        in_specs=[whole((rows, features)), out_spec(out_full)],
        out_specs=pl.BlockSpec((1, rows, width), lambda step: (step, 0, 0)),
        compiler_params=pltpu.CompilerParams(
            dimension_semantics=("arbitrary",), vmem_limit_bytes=24 << 20
        ),
        cost_estimate=pl.CostEstimate(
            flops=2 * rows * features * ranks * width,
            bytes_accessed=2 * ranks * width * features,
            transcendentals=0,
        ),
    )(grad_attn, out_full)


def feed_kernel(
    rows_ref,
    branch_ref,
    gate_ref,
    up_ref,
    down_ref,
    hidden_ref,
    gate_back_ref,
    up_back_ref,
    two_ref,
    mlp_ref,
    two_sum,
    mlp_sum,
):
    step = pl.program_id(0)

    @pl.when(step == 0)
    def _():
        two_sum[...] = jnp.zeros_like(two_sum)
        mlp_sum[...] = jnp.zeros_like(mlp_sum)

    rows = rows_ref[...]
    gate_pre = rows_by(rows, gate_ref[...], (1, 0))
    up_pre = rows_by(rows, up_ref[...], (1, 0))
    grad_hidden = rows_by(branch_ref[...], down_ref[...], (1, 1))
    scale, cube = 0.7978845608028654, 0.044715
    square = gate_pre * gate_pre
    bend = jnp.tanh(scale * (gate_pre + cube * (square * gate_pre)))
    half = 0.5 * (1.0 + bend)
    curved = gate_pre * half
    slope = half + (0.5 * scale) * gate_pre * (1.0 - bend * bend) * (1.0 + (3.0 * cube) * square)
    hidden = (curved * up_pre).astype(LOW)
    gate_back = (grad_hidden * up_pre * slope).astype(LOW)
    up_back = (grad_hidden * curved).astype(LOW)
    hidden_ref[...] = hidden
    gate_back_ref[...] = gate_back
    up_back_ref[...] = up_back
    two_sum[...] += rows_by(gate_back, gate_ref[...], (1, 1)) + rows_by(up_back, up_ref[...], (1, 1))
    mlp_sum[...] += rows_by(hidden, down_ref[...], (1, 0))

    @pl.when(step == pl.num_programs(0) - 1)
    def _():
        two_ref[...] = two_sum[...].astype(two_ref.dtype)
        mlp_ref[...] = mlp_sum[...].astype(mlp_ref.dtype)


def feed_forward(rows, branch, gate_weight, up_weight, down_weight, kind):
    count, features = rows.shape
    units = gate_weight.shape[1]
    tile = min(512, units)
    columns = pl.BlockSpec((features, tile), lambda step: (0, step))
    made = pl.BlockSpec((count, tile), lambda step: (0, step))
    return pl.pallas_call(
        feed_kernel,
        name="feed_forward",
        out_shape=(
            *[jax.ShapeDtypeStruct((count, units), LOW)] * 3,
            *[jax.ShapeDtypeStruct((count, features), kind)] * 2,
        ),
        grid=(units // tile,),
        in_specs=[
            whole((count, features)),
            whole((count, features)),
            columns,
            columns,
            pl.BlockSpec((tile, features), lambda step: (step, 0)),
        ],
        out_specs=[made] * 3 + [whole((count, features))] * 2,
        scratch_shapes=[pltpu.VMEM((count, features), F32)] * 2,
        compiler_params=pltpu.CompilerParams(
            dimension_semantics=("arbitrary",), vmem_limit_bytes=40 << 20
        ),
        cost_estimate=pl.CostEstimate(
            flops=12 * count * features * units,
            bytes_accessed=6 * features * units,
            transcendentals=count * units,
        ),
    )(rows, branch, gate_weight, up_weight, down_weight)


def inverse_rms(values):
    return lax.rsqrt(jnp.mean(values * values, axis=-1, keepdims=True) + EPS)


def normed_back(values, inverse, gain_vec, grad):
    unit = values * inverse
    scaled = grad * gain_vec
    grad_values = inverse * (scaled - unit * jnp.mean(scaled * unit, axis=-1, keepdims=True))
    return grad_values, jnp.sum(grad * unit, axis=0)


def hold(value):
    return lax.optimization_barrier(value)


def shards(
    tokens,
    cotangent,
    lengths,
    query_weight,
    key_weight,
    value_weight,
    out_weight,
    gate_weight,
    up_weight,
    down_weight,
    attn_gain,
    mlp_gain,
    memory_gate,
):
    ranks = lax.axis_size("mp")
    row_count = tokens.shape[0]
    width = query_weight.shape[1]
    heads = width // DK
    per_chunk = row_count // SEG
    rank = lax.axis_index("mp")
    pieces = range(ranks)
    place = jnp.stack([rank, lengths[0]]).astype(jnp.int32)
    live = (rank * row_count + jnp.arange(row_count) < lengths[0]).astype(F32)[:, None]
    share = jax.nn.sigmoid(memory_gate)

    features = tokens.shape[1]
    blocks = lax.axis_size("dp")
    near, far = singles(ranks), doubles(ranks)

    def product(left, right):
        return rows_by(left, right, (0, 0)).astype(LOW)

    inputs = tokens.astype(F32)
    inverse_one = inverse_rms(inputs)
    normed_one = (inputs * inverse_one * attn_gain).astype(LOW)
    slice_rows = width // blocks
    out_slice = lax.dynamic_slice_in_dim(
        out_weight, lax.axis_index("dp") * slice_rows, slice_rows, axis=0
    )
    qkv_weight = jnp.concatenate([query_weight, key_weight, value_weight], axis=1)

    def project(rows):
        return rows_by(rows, qkv_weight, (1, 0)).astype(LOW)

    one = gather_near(normed_one, "mp")
    out_slices = gather_near(out_slice, "mp")
    qkv = {0: project(one[0])}
    one, out_slices, qkv, qkv_weight = hold((one, out_slices, qkv, qkv_weight))

    one.update(gather_far(one, "mp"))
    out_slices.update(gather_far(out_slices, "mp"))
    qkv.update({p: project(one[p]) for p in near})
    upstream = cotangent.astype(F32)
    branch_mine = (upstream * live).astype(LOW)
    one, out_slices, qkv, branch_mine = hold((one, out_slices, qkv, branch_mine))
    out_full = lax.all_gather(
        jnp.stack([out_slices[p] for p in pieces]), "dp", axis=0, tiled=True
    )

    branch = gather_near(branch_mine, "mp")
    qkv.update({p: project(one[p]) for p in far})
    qkv = stacked(qkv)
    mixed, memories, normers = attend(qkv, place, share, per_chunk)
    one_blocks = relative_blocks(stacked(one), "dp")
    mixed, one_blocks = hold((mixed, one_blocks))

    mixed = swap_pieces(
        {p: mixed[p * row_count : (p + 1) * row_count] for p in pieces}, "mp"
    )
    mixed, branch, out_full = hold((mixed, branch, out_full))

    out_full = out_full.reshape(blocks, ranks, slice_rows, features)
    state, normed_two = out_project(mixed, out_full, tokens, mlp_gain, place)
    mixed = stacked(mixed, axis=1)

    hidden, gate_back, up_back, two_parts, mlp_parts = {}, {}, {}, {}, {}

    def feed(p):
        kind = LOW if p == 1 or p in far else F32
        hidden[p], gate_back[p], up_back[p], two_parts[p], mlp_parts[p] = feed_forward(
            two[p], branch[p], gate_weight, up_weight, down_weight, kind
        )

    two = gather_near(normed_two, "mp")
    branch.update(gather_far(branch, "mp"))
    feed(0)
    feed(1)
    two, hidden, gate_back, up_back, two_parts, mlp_parts, branch = hold(
        (two, hidden, gate_back, up_back, two_parts, mlp_parts, branch)
    )

    two.update(gather_far(two, "mp"))
    for p in near[1:]:
        feed(p)
    branch_blocks = relative_blocks(stacked(branch), "dp")
    two, hidden, gate_back, up_back, two_parts, mlp_parts, branch, branch_blocks = hold(
        (two, hidden, gate_back, up_back, two_parts, mlp_parts, branch, branch_blocks)
    )

    mlp_near = reduce_near(mlp_parts, None, "mp", (1,))
    for p in far:
        feed(p)
    two, hidden, gate_back, up_back, two_parts, mlp_parts, mlp_near = hold(
        (two, hidden, gate_back, up_back, two_parts, mlp_parts, mlp_near)
    )

    two_far = reduce_far(two_parts, "mp")
    all_two = stacked(two)
    gate_product = product(all_two, stacked(gate_back))
    all_hidden, all_up_back = stacked(hidden), stacked(up_back)
    two_parts, two_far, all_hidden, all_up_back, _ = hold(
        (two_parts, two_far, all_hidden, all_up_back, gate_product)
    )

    two_near = reduce_near(two_parts, two_far, "mp")
    up_product = product(all_two, all_up_back)
    down_products = [product(all_hidden, half) for half in branch_blocks]
    two_near, mlp_parts, down_products, _ = hold(
        (two_near, mlp_parts, down_products, up_product)
    )

    def spread(value, dim):
        return lax.psum_scatter(value, "dp", scatter_dimension=dim, tiled=True).astype(F32)

    grad_gate = spread(gate_product, 0)
    grad_up = spread(up_product, 0)

    mlp_far = reduce_far(mlp_parts, "mp")
    down_sum = BlockSum(*down_products, "dp", 1)
    grad_normed_two = total(two_parts[0], two_near)
    grad_through, grad_mlp_gain = normed_back(
        state, inverse_rms(state), mlp_gain, grad_normed_two
    )
    grad_state = upstream + grad_through
    grad_attn = (grad_state * live).astype(LOW)
    grad_mixed = out_back(grad_attn, out_full)
    grad_mixed = stacked(swap_pieces({p: grad_mixed[p] for p in pieces}, "mp"))
    out_products = [product(mixed, half) for half in relative_blocks(grad_attn, "dp")]
    out_sum = BlockSum(*out_products, "dp", 1)
    down_sum.step(0)
    mlp_far, grad_mixed, out_sum.state, down_sum.state, mlp_parts, grad_state, grad_mlp_gain = hold(
        (mlp_far, grad_mixed, out_sum.state, down_sum.state, mlp_parts, grad_state, grad_mlp_gain)
    )

    out_sum.step(0)
    for k in range(1, down_sum.steps):
        down_sum.step(k)
    mlp_near.update(reduce_near(mlp_parts, mlp_far, "mp", near[1:]))
    grad_qkv, grad_mix = attend_back(
        qkv, grad_mixed, memories, normers, place, share, per_chunk
    )
    grad_qkv, grad_mix, down_sum.state, out_sum.state = hold(
        (grad_qkv, grad_mix, down_sum.state, out_sum.state)
    )
    one_parts = {}

    def project_back(p):
        value = rows_by(grad_qkv[p * row_count : (p + 1) * row_count], qkv_weight, (1, 1))
        one_parts[p] = value.astype(LOW) if p == 1 or p in far else value

    for p in far:
        project_back(p)
    one_parts, grad_qkv = hold((one_parts, grad_qkv))
    one_far = reduce_far(one_parts, "mp")
    qkv_products = [product(half, grad_qkv) for half in one_blocks]
    qkv_sum = BlockSum(*qkv_products, "dp", 0)
    for k in range(1, out_sum.steps):
        out_sum.step(k)
    for p in [0] + near:
        project_back(p)
    grad_down = down_sum.result()
    one_parts, one_far, mlp_near, out_sum.state, qkv_sum.state, grad_down = hold(
        (one_parts, one_far, mlp_near, out_sum.state, qkv_sum.state, grad_down)
    )

    one_near = reduce_near(one_parts, one_far, "mp")
    block_out = (state + live * total(mlp_parts[0], mlp_near)).astype(LOW)
    grad_attn_gain = (
        sum(jnp.sum(one[p].astype(F32) * one_parts[p].astype(F32), axis=0) for p in pieces)
        / attn_gain
    )
    grad_share = jnp.sum(grad_mix, axis=1) * share * (1.0 - share)
    share_full = lax.dynamic_update_slice(
        jnp.zeros((heads * ranks,), F32), grad_share, (rank * heads,)
    )
    small = sum_everywhere(
        jnp.concatenate([grad_attn_gain, grad_mlp_gain, share_full]), ("mp", "dp")
    )
    for k in range(qkv_sum.steps):
        qkv_sum.step(k)
    grad_proj = qkv_sum.result()
    grad_out_part = out_sum.result()
    one_near, small, grad_proj, grad_out_part = hold((one_near, small, grad_proj, grad_out_part))

    grad_query, grad_key, grad_value = (
        grad_proj[:, j * width : (j + 1) * width] for j in range(3)
    )
    out_parts = {p: grad_out_part[p * width : (p + 1) * width] for p in pieces}
    grad_out = total(
        out_parts[0], {p: hop(out_parts[p].astype(LOW), "mp", p) for p in range(1, ranks)}
    )
    grad_normed_one = total(one_parts[0], one_near)
    grad_inputs = normed_back(inputs, inverse_one, attn_gain, grad_normed_one)[0]
    grad_tokens = grad_state + grad_inputs
    return (
        block_out,
        grad_tokens,
        grad_query,
        grad_key,
        grad_value,
        grad_out,
        grad_gate,
        grad_up,
        grad_down,
        small[:features],
        small[features : 2 * features],
        small[2 * features :],
    )


def solution(mesh):
    return jax.shard_map(
        shards,
        mesh=mesh,
        in_specs=(
            P(("dp", "mp"), None),
            P(("dp", "mp"), None),
            P("dp"),
            P(None, "mp"),
            P(None, "mp"),
            P(None, "mp"),
            P("mp", None),
            P(None, "mp"),
            P(None, "mp"),
            P("mp", None),
            P(),
            P(),
            P("mp"),
        ),
        out_specs=(
            P(("dp", "mp"), None),
            P(("dp", "mp"), None),
            P("dp", "mp"),
            P("dp", "mp"),
            P("dp", "mp"),
            P("mp", "dp"),
            P("dp", "mp"),
            P("dp", "mp"),
            P("mp", "dp"),
            P(),
            P(),
            P(),
        ),
        check_vma=False,
    )
```

```python
import functools

import jax
import jax.numpy as jnp
from jax import lax
from jax.experimental import pallas as pl
from jax.experimental.pallas import tpu as pltpu
from jax.sharding import PartitionSpec as P

DK = 128
SEG = 128
EPS = 1e-05
NEGATIVE = -1e30
LOW = jnp.bfloat16
F32 = jnp.float32
BRIEF = pl.CostEstimate(flops=1, bytes_accessed=1, transcendentals=0)


def hop(value, axis, mask):
    size = lax.axis_size(axis)
    return lax.ppermute(value, axis, [(j, j ^ mask) for j in range(size)])


def top_bit(number):
    return 1 << (number.bit_length() - 1)


def singles(size):
    return [p for p in range(1, size) if p == top_bit(p)]


def doubles(size):
    return [p for p in range(1, size) if p != top_bit(p)]


def gather_near(mine, axis):
    return {0: mine, **{p: hop(mine, axis, p) for p in singles(lax.axis_size(axis))}}


def gather_far(pieces, axis):
    size = lax.axis_size(axis)
    return {p: hop(pieces[top_bit(p)], axis, p ^ top_bit(p)) for p in doubles(size)}


def reduce_far(parts, axis):
    size = lax.axis_size(axis)
    return {p: hop(parts[p].astype(LOW), axis, p ^ top_bit(p)) for p in doubles(size)}


def reduce_near(parts, got, axis, only=None):
    size = lax.axis_size(axis)
    sent = {}
    for p in singles(size):
        if only is None or p in only:
            value = parts[p].astype(F32)
            for q in doubles(size):
                if top_bit(q) == p:
                    value = value + got[q].astype(F32)
            sent[p] = hop(value.astype(LOW), axis, p)
    return sent


def total(own, *arrived):
    value = own.astype(F32)
    for some in arrived:
        for p in some:
            value = value + some[p].astype(F32)
    return value


def swap_pieces(pieces, axis):
    return {p: hop(pieces[p], axis, p) if p else pieces[p] for p in range(lax.axis_size(axis))}


def stacked(pieces, axis=0):
    return jnp.concatenate([pieces[p] for p in range(len(pieces))], axis=axis)


def relative_blocks(value, axis):
    size = lax.axis_size(axis)
    mine = lax.axis_index(axis)
    step = value.shape[1] // size

    def take(r):
        return lax.dynamic_slice_in_dim(value, (mine ^ r) * step, step, axis=1)

    return (
        jnp.concatenate([take(r) for r in range(0, size, 2)], axis=1),
        jnp.concatenate([take(r) for r in range(1, size, 2)], axis=1),
    )


class DeviceSum:
    def __init__(self, parts, axis):
        self.keep, self.send = [parts[0], parts[2]], [parts[1], parts[3]]
        self.axis, self.turn = axis, 0
        self.flight = None

    def masks(self):
        return 2 << self.turn, (lax.axis_size(self.axis) // 2) >> self.turn

    def land(self):
        self.turn += 1
        for side in (0, 1):
            value = self.keep[side].astype(F32) + self.flight[side].astype(F32)
            half = value.shape[0] // 2
            if half and side == 0:
                self.keep[0], self.send[0] = value[0::2], value[1::2].astype(LOW)
            elif half:
                self.keep[1], self.send[1] = value[:half], value[half:].astype(LOW)
            else:
                self.keep[side] = value

    def result(self):
        return jnp.concatenate([value[0] for value in self.keep], axis=0)

    @property
    def state(self):
        return self.keep, self.send, self.flight

    @state.setter
    def state(self, value):
        self.keep, self.send, self.flight = value


def fly(*sums):
    groups = {}
    for one in sums:
        one.flight = [None, None]
        for side, mask in enumerate(one.masks()):
            groups.setdefault((mask, one.send[side].shape[-1]), []).append((one, side))
    for (mask, wide), parts in sorted(groups.items(), key=lambda item: item[0]):
        rows = [one.send[side].reshape(-1, wide) for one, side in parts]
        flight = hop(jnp.concatenate(rows, axis=0), sums[0].axis, mask)
        start = 0
        for (one, side), some in zip(parts, rows):
            end = start + some.shape[0]
            one.flight[side] = flight[start:end].reshape(one.send[side].shape)
            start = end


def device_steps(axis):
    return (lax.axis_size(axis) // 2).bit_length() - 1


def sum_everywhere(vector, axes):
    for axis in axes:
        bit = 1
        while bit < lax.axis_size(axis):
            vector = vector + hop(vector, axis, bit)
            bit *= 2
    return vector


def rows_by(left, right, contract, precision=None):
    return lax.dot_general(
        left, right, ((contract[:1], contract[1:]), ((), ())), preferred_element_type=F32
    )


def split(value):
    high = value.astype(LOW)
    return high, (value - high.astype(F32)).astype(LOW)


def fine(left, right, contract):
    (lh, ll), (rh, rl) = split(left), split(right)
    return (
        rows_by(lh, rh, contract) + rows_by(lh, rl, contract) + rows_by(ll, rh, contract)
    )


def lifted(values):
    return jnp.where(values > 0, values + 1.0, jnp.exp(jnp.minimum(values, 0.0)))


def lifted_slope(values):
    slope = jnp.exp(jnp.minimum(values, 0.0))
    return jnp.where(values > 0, 1.0, jnp.where(values < 0, slope, 0.5))


def probabilities(queries, key_rows):
    scores = rows_by(queries, key_rows, (1, 1)) * DK ** (-0.5)
    row = lax.broadcasted_iota(jnp.int32, (SEG, SEG), 0)
    col = lax.broadcasted_iota(jnp.int32, (SEG, SEG), 1)
    scores = jnp.where(row >= col, scores, NEGATIVE)
    lift = jnp.exp(scores - jnp.max(scores, axis=-1, keepdims=True))
    return lift / jnp.sum(lift, axis=-1, keepdims=True)


def live_column(segment, length):
    position = segment * SEG + lax.broadcasted_iota(jnp.int32, (SEG, 1), 0)
    return (position < length).astype(F32)


def attend_kernel(place, share, qkv_ref, mixed_ref, memory_ref, normer_ref, memory, normer):
    heads = memory.shape[0]
    width = heads * DK
    segment = pl.program_id(0)

    @pl.when(segment == 0)
    def _():
        memory[...] = jnp.zeros_like(memory)
        normer[...] = jnp.ones_like(normer)

    live = live_column(segment, place[1])
    memory_ref[0] = memory[...]
    normer_ref[0] = normer[...]
    for h in range(heads):
        at = h * DK
        queries = qkv_ref[:, at : at + DK]
        key_rows = qkv_ref[:, width + at : width + at + DK]
        value_rows = qkv_ref[:, 2 * width + at : 2 * width + at + DK]
        probs = probabilities(queries, key_rows).astype(LOW)
        in_block = rows_by(probs, value_rows, (1, 0))
        lifted_q = lifted(queries.astype(F32))
        lifted_k = lifted(key_rows.astype(F32))
        held = memory[h]
        norm = normer[h : h + 1]
        read = fine(jnp.concatenate([lifted_q, lifted_k], axis=0), held, (1, 0))
        recalled = read[:SEG] / jnp.sum(lifted_q * norm, axis=-1, keepdims=True)
        guessed = read[SEG:] / jnp.sum(lifted_k * norm, axis=-1, keepdims=True)
        mix = share[h]
        mixed_ref[:, at : at + DK] = (mix * recalled + (1.0 - mix) * in_block).astype(LOW)
        written = lifted_k * live
        memory[h] = held + fine(written, value_rows.astype(F32) - guessed, (0, 0))
        normer[h : h + 1] = norm + jnp.sum(written, axis=0, keepdims=True)


def attend_back_kernel(
    place, share, qkv_ref, grad_ref, memory_ref, normer_ref, out_ref, mix_ref, grad_memory, grad_normer
):
    heads = grad_memory.shape[0]
    width = heads * DK
    step = pl.program_id(0)
    segment = pl.num_programs(0) - 1 - step

    @pl.when(step == 0)
    def _():
        grad_memory[...] = jnp.zeros_like(grad_memory)
        grad_normer[...] = jnp.zeros_like(grad_normer)
        mix_ref[...] = jnp.zeros_like(mix_ref)

    live = live_column(segment, place[1])
    for h in range(heads):
        at = h * DK
        queries = qkv_ref[:, at : at + DK]
        key_rows = qkv_ref[:, width + at : width + at + DK]
        value_rows = qkv_ref[:, 2 * width + at : 2 * width + at + DK]
        grad_mixed = grad_ref[:, at : at + DK].astype(F32)
        mix = share[h]
        probs = probabilities(queries, key_rows)
        probs_low = probs.astype(LOW)
        in_block = rows_by(probs_low, value_rows, (1, 0))
        grad_local = ((1.0 - mix) * grad_mixed).astype(LOW)
        back_v = rows_by(probs_low, grad_local, (0, 0))
        grad_probs = rows_by(grad_local, value_rows, (1, 1))
        inner = jnp.sum(grad_probs * probs, axis=-1, keepdims=True)
        grad_scores = (probs * (grad_probs - inner)).astype(LOW)
        back_q = rows_by(grad_scores, key_rows, (1, 0)) * DK ** (-0.5)
        back_k = rows_by(grad_scores, queries, (0, 0)) * DK ** (-0.5)
        float_q = queries.astype(F32)
        float_k = key_rows.astype(F32)
        lifted_q = lifted(float_q)
        lifted_k = lifted(float_k)
        both = jnp.concatenate([lifted_q, lifted_k], axis=0)
        held = memory_ref[0, h]
        norm = normer_ref[0, h : h + 1]
        over_q = 1.0 / jnp.sum(lifted_q * norm, axis=-1, keepdims=True)
        over_k = 1.0 / jnp.sum(lifted_k * norm, axis=-1, keepdims=True)
        read = fine(both, held, (1, 0))
        recalled = read[:SEG] * over_q
        guessed = read[SEG:] * over_k
        mix_ref[h : h + 1] += jnp.sum(
            grad_mixed * (recalled - in_block), axis=0, keepdims=True
        )
        grad_held = grad_memory[h]
        grad_norm = grad_normer[h : h + 1]
        written = lifted_k * live
        grad_update = fine(written, grad_held, (1, 0))
        grad_written = fine(value_rows.astype(F32) - guessed, grad_held, (1, 1)) + grad_norm
        grad_recalled = mix * grad_mixed
        grad_read_q = grad_recalled * over_q
        grad_read_k = -grad_update * over_k
        grad_sum_q = -jnp.sum(grad_read_q * recalled, axis=-1, keepdims=True)
        grad_sum_k = -jnp.sum(grad_read_k * guessed, axis=-1, keepdims=True)
        grad_reads = jnp.concatenate([grad_read_q, grad_read_k], axis=0)
        back = fine(grad_reads, held, (1, 1))
        grad_lifted_q = back[:SEG] + grad_sum_q * norm
        grad_lifted_k = back[SEG:] + grad_sum_k * norm + live * grad_written
        grad_memory[h] = grad_held + fine(both, grad_reads, (0, 0))
        grad_normer[h : h + 1] = grad_norm + jnp.sum(
            lifted_q * grad_sum_q + lifted_k * grad_sum_k, axis=0, keepdims=True
        )
        out_ref[:, at : at + DK] = (back_q + grad_lifted_q * lifted_slope(float_q)).astype(LOW)
        out_ref[:, width + at : width + at + DK] = (
            back_k + grad_lifted_k * lifted_slope(float_k)
        ).astype(LOW)
        out_ref[:, 2 * width + at : 2 * width + at + DK] = (back_v + grad_update).astype(LOW)


def segment_place(segment, place, per_chunk):
    chunk = lax.div(segment, per_chunk) ^ place[0]
    return chunk * per_chunk + lax.rem(segment, per_chunk)


def attend(qkv, place, share, per_chunk):
    rows, wide = qkv.shape
    heads = wide // (3 * DK)
    blocks = rows // SEG

    def row_map(step, place):
        return (segment_place(step, place, per_chunk), 0)

    return pl.pallas_call(
        attend_kernel,
        name="attend",
        out_shape=(
            jax.ShapeDtypeStruct((rows, heads * DK), LOW),
            jax.ShapeDtypeStruct((blocks, heads, DK, DK), F32),
            jax.ShapeDtypeStruct((blocks, heads, DK), F32),
        ),
        grid_spec=pltpu.PrefetchScalarGridSpec(
            num_scalar_prefetch=1,
            grid=(blocks,),
            in_specs=[
                pl.BlockSpec(memory_space=pltpu.SMEM),
                pl.BlockSpec((SEG, wide), row_map),
            ],
            out_specs=[
                pl.BlockSpec((SEG, heads * DK), row_map),
                pl.BlockSpec((1, heads, DK, DK), lambda step, place: (step, 0, 0, 0)),
                pl.BlockSpec((1, heads, DK), lambda step, place: (step, 0, 0)),
            ],
            scratch_shapes=[pltpu.VMEM((heads, DK, DK), F32), pltpu.VMEM((heads, DK), F32)],
        ),
        compiler_params=pltpu.CompilerParams(
            dimension_semantics=("arbitrary",), vmem_limit_bytes=24 << 20
        ),
        cost_estimate=BRIEF,
    )(place, share, qkv)


def attend_back(qkv, grad_mixed, memories, normers, place, share, per_chunk):
    rows, wide = qkv.shape
    heads = wide // (3 * DK)
    blocks = rows // SEG

    def row_map(step, place):
        return (segment_place(blocks - 1 - step, place, per_chunk), 0)

    return pl.pallas_call(
        attend_back_kernel,
        name="attend_back",
        out_shape=(
            jax.ShapeDtypeStruct((rows, wide), LOW),
            jax.ShapeDtypeStruct((heads, DK), F32),
        ),
        grid_spec=pltpu.PrefetchScalarGridSpec(
            num_scalar_prefetch=1,
            grid=(blocks,),
            in_specs=[
                pl.BlockSpec(memory_space=pltpu.SMEM),
                pl.BlockSpec((SEG, wide), row_map),
                pl.BlockSpec((SEG, heads * DK), row_map),
                pl.BlockSpec(
                    (1, heads, DK, DK), lambda step, place: (blocks - 1 - step, 0, 0, 0)
                ),
                pl.BlockSpec((1, heads, DK), lambda step, place: (blocks - 1 - step, 0, 0)),
            ],
            out_specs=[
                pl.BlockSpec((SEG, wide), row_map),
                pl.BlockSpec((heads, DK), lambda step, place: (0, 0)),
            ],
            scratch_shapes=[pltpu.VMEM((heads, DK, DK), F32), pltpu.VMEM((heads, DK), F32)],
        ),
        compiler_params=pltpu.CompilerParams(
            dimension_semantics=("arbitrary",), vmem_limit_bytes=24 << 20
        ),
        cost_estimate=pl.CostEstimate(
            flops=blocks * heads * 240 * SEG**3,
            bytes_accessed=rows * wide * 6,
            transcendentals=0,
        ),
    )(place, share, qkv, grad_mixed, memories, normers)


def live_rows(place, rows):
    position = place[0] * rows + lax.broadcasted_iota(jnp.int32, (rows, 1), 0)
    return (position < place[1]).astype(F32)


def out_project_kernel(place, *refs):
    *mixed_refs, out_ref, tokens_ref, gain_ref, state_ref, normed_ref = refs
    step = pl.program_id(0)

    @pl.when(step == 0)
    def _():
        state_ref[...] = jnp.zeros_like(state_ref)

    weight = out_ref[...].reshape(-1, out_ref.shape[-1])
    for k, mixed_ref in enumerate(mixed_refs):

        @pl.when(step == k)
        def _():
            state_ref[...] += rows_by(mixed_ref[...], weight, (1, 0))

    @pl.when(step == len(mixed_refs) - 1)
    def _():
        live = live_rows(place, state_ref.shape[0])
        state = tokens_ref[...].astype(F32) + live * state_ref[...]
        state_ref[...] = state
        normed_ref[...] = (state * inverse_rms(state) * gain_ref[...]).astype(LOW)


def out_spec(out_full):
    blocks, _, rows, features = out_full.shape
    return pl.BlockSpec((blocks, 1, rows, features), lambda step, *_: (0, step, 0, 0))


def whole(shape):
    return pl.BlockSpec(shape, lambda *_: (0,) * len(shape))


def out_project(mixed, out_full, tokens, gain, place):
    ranks = len(mixed)
    rows, features = tokens.shape
    width = mixed[0].shape[1]
    return pl.pallas_call(
        out_project_kernel,
        name="out_project",
        out_shape=(
            jax.ShapeDtypeStruct((rows, features), F32),
            jax.ShapeDtypeStruct((rows, features), LOW),
        ),
        grid_spec=pltpu.PrefetchScalarGridSpec(
            num_scalar_prefetch=1,
            grid=(ranks,),
            in_specs=[whole((rows, width))] * ranks
            + [out_spec(out_full), whole((rows, features)), whole((1, features))],
            out_specs=[whole((rows, features))] * 2,
        ),
        compiler_params=pltpu.CompilerParams(
            dimension_semantics=("arbitrary",), vmem_limit_bytes=24 << 20
        ),
        cost_estimate=BRIEF,
    )(place, *[mixed[p] for p in range(ranks)], out_full, tokens, gain[None])


def out_back_kernel(grad_ref, out_ref, back_ref):
    weight = out_ref[...].reshape(-1, out_ref.shape[-1])
    back_ref[0] = rows_by(grad_ref[...], weight, (1, 1)).astype(LOW)


def out_back(grad_attn, out_full):
    rows, features = grad_attn.shape
    blocks, ranks, slice_rows, _ = out_full.shape
    width = blocks * slice_rows
    return pl.pallas_call(
        out_back_kernel,
        name="out_back",
        out_shape=jax.ShapeDtypeStruct((ranks, rows, width), LOW),
        grid=(ranks,),
        in_specs=[whole((rows, features)), out_spec(out_full)],
        out_specs=pl.BlockSpec((1, rows, width), lambda step: (step, 0, 0)),
        compiler_params=pltpu.CompilerParams(
            dimension_semantics=("arbitrary",), vmem_limit_bytes=24 << 20
        ),
        cost_estimate=BRIEF,
    )(grad_attn, out_full)


def feed_kernel(
    place,
    rows_ref,
    branch_ref,
    gate_ref,
    up_ref,
    down_ref,
    made_ref,
    kept_ref,
    sent_ref,
    two_ref,
    mlp_ref,
    two_sum,
    mlp_sum,
):
    step = pl.program_id(0)

    @pl.when(step == 0)
    def _():
        two_sum[...] = jnp.zeros_like(two_sum)
        mlp_sum[...] = jnp.zeros_like(mlp_sum)
        size = lax.axis_size("dp")
        block = rows_ref.shape[1] // size
        for k, source in enumerate((rows_ref, branch_ref)):
            for r in range(size):
                start = pl.multiple_of((place[2] ^ r) * block, block)
                target = sent_ref if r % 2 else kept_ref
                at = r // 2 * block
                target[k, :, at : at + block] = source[:, pl.ds(start, block)]

    rows = rows_ref[...]
    gate_pre = rows_by(rows, gate_ref[...], (1, 0))
    up_pre = rows_by(rows, up_ref[...], (1, 0))
    grad_hidden = rows_by(branch_ref[...], down_ref[...], (1, 1))
    scale, cube = 0.7978845608028654, 0.044715
    square = gate_pre * gate_pre
    bend = jnp.tanh(scale * (gate_pre + cube * (square * gate_pre)))
    half = 0.5 * (1.0 + bend)
    curved = gate_pre * half
    slope = half + (0.5 * scale) * gate_pre * (1.0 - bend * bend) * (1.0 + (3.0 * cube) * square)
    hidden = (curved * up_pre).astype(LOW)
    gate_back = (grad_hidden * up_pre * slope).astype(LOW)
    up_back = (grad_hidden * curved).astype(LOW)
    made_ref[0] = hidden
    made_ref[1] = gate_back
    made_ref[2] = up_back
    two_sum[...] += rows_by(gate_back, gate_ref[...], (1, 1)) + rows_by(up_back, up_ref[...], (1, 1))
    mlp_sum[...] += rows_by(hidden, down_ref[...], (1, 0))

    @pl.when(step == pl.num_programs(0) - 1)
    def _():
        two_ref[...] = two_sum[...].astype(two_ref.dtype)
        mlp_ref[...] = mlp_sum[...].astype(mlp_ref.dtype)


def feed_forward(rows, branch, gate_weight, up_weight, down_weight, place, kind):
    count, features = rows.shape
    units = gate_weight.shape[1]
    tile = min(512, units)
    columns = pl.BlockSpec((features, tile), lambda step, place: (0, step))
    half = (2, count, features // 2)
    return pl.pallas_call(
        feed_kernel,
        name="feed_forward",
        out_shape=(
            jax.ShapeDtypeStruct((3, count, units), LOW),
            *[jax.ShapeDtypeStruct(half, LOW)] * 2,
            *[jax.ShapeDtypeStruct((count, features), kind)] * 2,
        ),
        grid_spec=pltpu.PrefetchScalarGridSpec(
            num_scalar_prefetch=1,
            grid=(units // tile,),
            in_specs=[
                whole((count, features)),
                whole((count, features)),
                columns,
                columns,
                pl.BlockSpec((tile, features), lambda step, place: (step, 0)),
            ],
            out_specs=[
                pl.BlockSpec((3, count, tile), lambda step, place: (0, 0, step)),
                *[whole(half)] * 2,
                *[whole((count, features))] * 2,
            ],
            scratch_shapes=[pltpu.VMEM((count, features), F32)] * 2,
        ),
        compiler_params=pltpu.CompilerParams(
            dimension_semantics=("arbitrary",), vmem_limit_bytes=44 << 20
        ),
        cost_estimate=BRIEF,
    )(place, rows, branch, gate_weight, up_weight, down_weight)


def project_back_kernel(*refs):
    count = (len(refs) - 2) // 3
    rows_refs, one_refs, weight_ref = refs[:count], refs[count : 2 * count], refs[2 * count]
    out_refs, gain_ref = refs[2 * count + 1 : -1], refs[-1]
    weight = weight_ref[...]
    gain = jnp.zeros(gain_ref.shape, F32)
    for rows_ref, one_ref, out_ref in zip(rows_refs, one_refs, out_refs):
        value = rows_by(rows_ref[...], weight, (1, 1))
        out_ref[...] = value.astype(out_ref.dtype)
        gain = gain + jnp.sum(value * one_ref[...].astype(F32), axis=0, keepdims=True)
    gain_ref[...] = gain


def project_rows_back(rows, weight, count, one, wanted, kinds):
    features, wide = weight.shape
    tile = min(512, features)
    made = pl.BlockSpec((count, tile), lambda step: (0, step))
    *parts, gain = pl.pallas_call(
        project_back_kernel,
        name="project_back",
        out_shape=[jax.ShapeDtypeStruct((count, features), kind) for kind in kinds]
        + [jax.ShapeDtypeStruct((1, features), F32)],
        grid=(features // tile,),
        in_specs=[pl.BlockSpec((count, wide), lambda step, p=p: (p, 0)) for p in wanted]
        + [made] * len(wanted)
        + [pl.BlockSpec((tile, wide), lambda step: (step, 0))],
        out_specs=[made] * len(wanted) + [pl.BlockSpec((1, tile), lambda step: (0, step))],
        compiler_params=pltpu.CompilerParams(
            dimension_semantics=("arbitrary",), vmem_limit_bytes=24 << 20
        ),
        cost_estimate=BRIEF,
    )(*[rows] * len(wanted), *[one[p] for p in wanted], weight)
    return dict(zip(wanted, parts)), gain[0]


def weight_kernel(*refs):
    *in_refs, low_keep, low_send, high_keep, high_send = refs
    half = len(in_refs) // 2
    step = pl.program_id(0)
    steps = pl.num_programs(0)
    value = rows_by(in_refs[0][...], in_refs[half][...], (0, 0))
    for left, right in zip(in_refs[1:half], in_refs[half + 1 :]):
        value = value + rows_by(left[...], right[...], (0, 0))
    value = value.astype(LOW)
    middle = value.shape[0] // 2
    odd = lax.rem(step, 2) == 1
    upper = step >= steps // 2

    @pl.when(jnp.logical_not(odd))
    def _():
        low_keep[...] = value[:middle]

    @pl.when(odd)
    def _():
        low_send[...] = value[:middle]

    @pl.when(jnp.logical_not(upper))
    def _():
        high_keep[...] = value[middle:]

    @pl.when(upper)
    def _():
        high_send[...] = value[middle:]


def weight_blocks(lefts, rights, blocks):
    across = lefts[0][0].shape[2] // blocks
    along = rights[0][0].shape[2]

    def left_spec(pair):
        return pl.BlockSpec((None, pair[0].shape[1], across), lambda step: (pair[1], 0, step))

    def right_spec(pair):
        return pl.BlockSpec((None, pair[0].shape[1], along), lambda step: (pair[1], 0, 0))

    def out_spec_of(place):
        return pl.BlockSpec((None, across // 2, along), lambda step: (place(step), 0, 0))

    half = blocks // 2
    return pl.pallas_call(
        weight_kernel,
        name="weight_blocks",
        out_shape=[jax.ShapeDtypeStruct((half, across // 2, along), LOW)] * 4,
        grid=(blocks,),
        in_specs=[left_spec(pair) for pair in lefts] + [right_spec(pair) for pair in rights],
        out_specs=[
            out_spec_of(lambda step: lax.div(step, 2)),
            out_spec_of(lambda step: lax.div(step, 2)),
            out_spec_of(lambda step: jnp.minimum(step, half - 1)),
            out_spec_of(lambda step: jnp.maximum(step - half, 0)),
        ],
        compiler_params=pltpu.CompilerParams(
            dimension_semantics=("arbitrary",), vmem_limit_bytes=40 << 20
        ),
        cost_estimate=BRIEF,
    )(*[pair[0] for pair in lefts], *[pair[0] for pair in rights])


def inverse_rms(values):
    return lax.rsqrt(jnp.mean(values * values, axis=-1, keepdims=True) + EPS)


def normed_back(values, inverse, gain_vec, grad):
    unit = values * inverse
    scaled = grad * gain_vec
    grad_values = inverse * (scaled - unit * jnp.mean(scaled * unit, axis=-1, keepdims=True))
    return grad_values, jnp.sum(grad * unit, axis=0)


def hold(value):
    return lax.optimization_barrier(value)


def shards(
    tokens,
    cotangent,
    lengths,
    query_weight,
    key_weight,
    value_weight,
    out_weight,
    gate_weight,
    up_weight,
    down_weight,
    attn_gain,
    mlp_gain,
    memory_gate,
):
    ranks = lax.axis_size("mp")
    row_count = tokens.shape[0]
    width = query_weight.shape[1]
    heads = width // DK
    per_chunk = row_count // SEG
    rank = lax.axis_index("mp")
    pieces = range(ranks)
    place = jnp.stack([rank, lengths[0], lax.axis_index("dp")]).astype(jnp.int32)
    live = (rank * row_count + jnp.arange(row_count) < lengths[0]).astype(F32)[:, None]
    share = jax.nn.sigmoid(memory_gate)

    features = tokens.shape[1]
    blocks = lax.axis_size("dp")
    near, far = singles(ranks), doubles(ranks)

    def product(left, right):
        return rows_by(left, right, (0, 0)).astype(LOW)

    inputs = tokens.astype(F32)
    inverse_one = inverse_rms(inputs)
    normed_one = (inputs * inverse_one * attn_gain).astype(LOW)
    slice_rows = width // blocks
    out_slice = lax.dynamic_slice_in_dim(
        out_weight, lax.axis_index("dp") * slice_rows, slice_rows, axis=0
    )
    out_slice, normed_one = hold((out_slice, normed_one))
    qkv_weight = jnp.concatenate([query_weight, key_weight, value_weight], axis=1)

    def project(rows):
        return rows_by(rows, qkv_weight, (1, 0)).astype(LOW)

    one = gather_near(normed_one, "mp")
    out_slices = gather_near(out_slice, "mp")
    qkv = {0: project(one[0])}
    one, out_slices, qkv, qkv_weight = hold((one, out_slices, qkv, qkv_weight))

    one.update(gather_far(one, "mp"))
    out_slices.update(gather_far(out_slices, "mp"))
    qkv.update({p: project(one[p]) for p in near})
    upstream = cotangent.astype(F32)
    branch_mine = (upstream * live).astype(LOW)
    one, out_slices, qkv, branch_mine = hold((one, out_slices, qkv, branch_mine))
    out_full = lax.all_gather(
        jnp.stack([out_slices[p] for p in pieces]), "dp", axis=0, tiled=True
    )

    branch = gather_near(branch_mine, "mp")
    qkv.update({p: project(one[p]) for p in far})
    qkv = stacked(qkv)
    mixed, memories, normers = attend(qkv, place, share, per_chunk)
    mixed = hold(mixed)

    mixed = swap_pieces(
        {p: mixed[p * row_count : (p + 1) * row_count] for p in pieces}, "mp"
    )
    mixed, branch = hold((mixed, branch))

    out_full = out_full.reshape(blocks, ranks, slice_rows, features)
    state, normed_two = out_project(mixed, out_full, tokens, mlp_gain, place)
    mixed = stacked(mixed, axis=1)

    made, kept, sent, two_parts, mlp_parts = {}, {}, {}, {}, {}

    def feed(p):
        kind = LOW if p == 1 or p in far else F32
        made[p], kept[p], sent[p], two_parts[p], mlp_parts[p] = feed_forward(
            two[p], branch[p], gate_weight, up_weight, down_weight, place, kind
        )

    their_made, their_kept = {}, {}

    def share_rows(p):
        their_made[p] = hop(made[p], "dp", 1)
        their_kept[p] = hop(sent[p], "dp", 1)

    two = gather_near(normed_two, "mp")
    branch.update(gather_far(branch, "mp"))
    feed(0)
    one_kept, one_sent = relative_blocks(stacked(one), "dp")
    their_mixed = hop(mixed, "dp", 1)
    two, made, kept, sent, two_parts, mlp_parts, branch, one_kept, one_sent, their_mixed = hold(
        (two, made, kept, sent, two_parts, mlp_parts, branch, one_kept, one_sent, their_mixed)
    )

    two.update(gather_far(two, "mp"))
    share_rows(0)
    their_one = hop(one_sent, "dp", 1)
    feed(1)
    two, made, kept, sent, two_parts, mlp_parts, their_made, their_kept, their_one = hold(
        (two, made, kept, sent, two_parts, mlp_parts, their_made, their_kept, their_one)
    )

    mlp_near = reduce_near(mlp_parts, None, "mp", (1,))
    share_rows(1)
    for p in far:
        feed(p)
    two, made, kept, sent, two_parts, mlp_parts, their_made, their_kept, mlp_near = hold(
        (two, made, kept, sent, two_parts, mlp_parts, their_made, their_kept, mlp_near)
    )

    two_far = reduce_far(two_parts, "mp")
    for p in far:
        share_rows(p)
    for p in near[1:]:
        feed(p)
    made, kept, sent, two_parts, mlp_parts, their_made, their_kept, two_far = hold(
        (made, kept, sent, two_parts, mlp_parts, their_made, their_kept, two_far)
    )

    steps = device_steps("dp")

    def weights_of(left, right):
        return DeviceSum(
            weight_blocks(
                [(kept[p], left) for p in pieces] + [(their_kept[p], left) for p in pieces],
                [(made[p], right) for p in pieces] + [(their_made[p], right) for p in pieces],
                blocks // 2,
            ),
            "dp",
        )

    two_near = reduce_near(two_parts, two_far, "mp")
    for p in near[1:]:
        share_rows(p)
    gate_sum = weights_of(0, 1)
    fly(gate_sum)
    up_sum = weights_of(0, 2)
    two_near, mlp_parts, gate_sum.state, up_sum.state, made, kept, their_made, their_kept = hold(
        (two_near, mlp_parts, gate_sum.state, up_sum.state, made, kept, their_made, their_kept)
    )

    mlp_far = reduce_far(mlp_parts, "mp")
    fly(up_sum)
    grad_normed_two = total(two_parts[0], two_near)
    grad_through, grad_mlp_gain = normed_back(
        state, inverse_rms(state), mlp_gain, grad_normed_two
    )
    grad_state = upstream + grad_through
    grad_attn = (grad_state * live).astype(LOW)
    grad_mixed = out_back(grad_attn, out_full)
    attn_kept, attn_sent = relative_blocks(grad_attn, "dp")
    their_attn = hop(attn_sent, "dp", 1)
    down_sum = weights_of(1, 0)
    (
        mlp_far, grad_mixed, attn_kept, their_attn, grad_state, grad_mlp_gain, mlp_parts,
        gate_sum.state, up_sum.state, down_sum.state,
    ) = hold(
        (
            mlp_far, grad_mixed, attn_kept, their_attn, grad_state, grad_mlp_gain, mlp_parts,
            gate_sum.state, up_sum.state, down_sum.state,
        )
    )
    grad_mixed = stacked(swap_pieces({p: grad_mixed[p] for p in pieces}, "mp"))
    fly(down_sum)
    out_sum = DeviceSum(
        weight_blocks(
            [(attn_kept[None], 0), (their_attn[None], 0)],
            [(mixed[None], 0), (their_mixed[None], 0)],
            blocks // 2,
        ),
        "dp",
    )
    gate_sum.land()
    up_sum.land()
    grad_mixed, mlp_parts, gate_sum.state, up_sum.state, down_sum.state, out_sum.state = hold(
        (grad_mixed, mlp_parts, gate_sum.state, up_sum.state, down_sum.state, out_sum.state)
    )

    mlp_near.update(reduce_near(mlp_parts, mlp_far, "mp", near[1:]))
    fly(out_sum, *([gate_sum, up_sum] if steps > 1 else []))
    down_sum.land()
    grad_qkv, grad_mix = attend_back(
        qkv, grad_mixed, memories, normers, place, share, per_chunk
    )
    grad_qkv, grad_mix, mlp_near, out_sum.state, down_sum.state, gate_sum.state, up_sum.state = hold(
        (grad_qkv, grad_mix, mlp_near, out_sum.state, down_sum.state, gate_sum.state, up_sum.state)
    )

    def project_back(wanted):
        kinds = [LOW if p == 1 or p in far else F32 for p in wanted]
        return project_rows_back(grad_qkv, qkv_weight, row_count, one, wanted, kinds)

    their_qkv = hop(grad_qkv, "dp", 1)
    one_parts, gain_far = project_back(far)
    one_parts, grad_qkv, out_sum.state, down_sum.state, mlp_near = hold(
        (one_parts, grad_qkv, out_sum.state, down_sum.state, mlp_near)
    )
    one_far = reduce_far(one_parts, "mp")
    qkv_sum = DeviceSum(
        weight_blocks(
            [(one_kept[None], 0), (their_one[None], 0)],
            [(grad_qkv[None], 0), (their_qkv[None], 0)],
            blocks // 2,
        ),
        "dp",
    )
    grad_qkv, qkv_sum.state, out_sum.state, down_sum.state = hold(
        (grad_qkv, qkv_sum.state, out_sum.state, down_sum.state)
    )
    out_sum.land()
    if steps > 1:
        fly(down_sum, out_sum)
    more_parts, gain_near = project_back([0] + near)
    one_parts.update(more_parts)
    one_parts, one_far, qkv_sum.state, mlp_near = hold(
        (one_parts, one_far, qkv_sum.state, mlp_near)
    )

    one_near = reduce_near(one_parts, one_far, "mp")
    block_out = (state + live * total(mlp_parts[0], mlp_near)).astype(LOW)
    grad_attn_gain = (gain_far + gain_near) / attn_gain
    grad_share = jnp.sum(grad_mix, axis=1) * share * (1.0 - share)
    share_full = lax.dynamic_update_slice(
        jnp.zeros((heads * ranks,), F32), grad_share, (rank * heads,)
    )
    small = jnp.concatenate([grad_attn_gain, grad_mlp_gain, share_full])
    fly(qkv_sum)
    for k in range(1, steps):
        for some in ([gate_sum, up_sum], [down_sum, out_sum]):
            for one_sum in some:
                one_sum.land()
            if k + 1 < steps:
                fly(*some)
        qkv_sum.land()
        fly(qkv_sum)
    qkv_sum.land()
    grad_gate, grad_up = gate_sum.result(), up_sum.result()
    grad_down = down_sum.result().T
    grad_proj = qkv_sum.result()
    grad_out_part = out_sum.result()
    out_parts = {p: grad_out_part[:, p * width : (p + 1) * width] for p in pieces}
    out_parts = {p: out_parts[p].astype(LOW) if p else out_parts[p] for p in pieces}
    one_near, small, out_parts, block_out, grad_gate, grad_up, grad_down, grad_proj = hold(
        (one_near, small, out_parts, block_out, grad_gate, grad_up, grad_down, grad_proj)
    )

    small = sum_everywhere(small, ("mp", "dp"))
    grad_query, grad_key, grad_value = (
        grad_proj[:, j * width : (j + 1) * width] for j in range(3)
    )
    grad_out = total(
        out_parts[0], {p: hop(out_parts[p], "mp", p) for p in range(1, ranks)}
    ).T
    grad_normed_one = total(one_parts[0], one_near)
    grad_inputs = normed_back(inputs, inverse_one, attn_gain, grad_normed_one)[0]
    grad_tokens = grad_state + grad_inputs
    return (
        block_out,
        grad_tokens,
        grad_query,
        grad_key,
        grad_value,
        grad_out,
        grad_gate,
        grad_up,
        grad_down,
        small[:features],
        small[features : 2 * features],
        small[2 * features :],
    )


def solution(mesh):
    return jax.shard_map(
        shards,
        mesh=mesh,
        in_specs=(
            P(("dp", "mp"), None),
            P(("dp", "mp"), None),
            P("dp"),
            P(None, "mp"),
            P(None, "mp"),
            P(None, "mp"),
            P("mp", None),
            P(None, "mp"),
            P(None, "mp"),
            P("mp", None),
            P(),
            P(),
            P("mp"),
        ),
        out_specs=(
            P(("dp", "mp"), None),
            P(("dp", "mp"), None),
            P("dp", "mp"),
            P("dp", "mp"),
            P("dp", "mp"),
            P("mp", "dp"),
            P("dp", "mp"),
            P("dp", "mp"),
            P("mp", "dp"),
            P(),
            P(),
            P(),
        ),
        check_vma=False,
    )
```

```python
import functools

import jax
import jax.numpy as jnp
from jax import lax
from jax.experimental import pallas as pl
from jax.experimental.pallas import tpu as pltpu
from jax.sharding import PartitionSpec as P

DK = 128
SEG = 128
EPS = 1e-05
NEGATIVE = -1e30
LOW = jnp.bfloat16
F32 = jnp.float32
BRIEF = pl.CostEstimate(flops=1, bytes_accessed=1, transcendentals=0)


def hop(value, axis, mask):
    size = lax.axis_size(axis)
    return lax.ppermute(value, axis, [(j, j ^ mask) for j in range(size)])


def top_bit(number):
    return 1 << (number.bit_length() - 1)


def singles(size):
    return [p for p in range(1, size) if p == top_bit(p)]


def doubles(size):
    return [p for p in range(1, size) if p != top_bit(p)]


def gather_near(mine, axis):
    return {0: mine, **{p: hop(mine, axis, p) for p in singles(lax.axis_size(axis))}}


def gather_far(pieces, axis):
    size = lax.axis_size(axis)
    return {p: hop(pieces[top_bit(p)], axis, p ^ top_bit(p)) for p in doubles(size)}


def reduce_far(parts, axis):
    size = lax.axis_size(axis)
    return {p: hop(parts[p].astype(LOW), axis, p ^ top_bit(p)) for p in doubles(size)}


def reduce_near(parts, got, axis, only=None):
    size = lax.axis_size(axis)
    sent = {}
    for p in singles(size):
        if only is None or p in only:
            value = parts[p].astype(F32)
            for q in doubles(size):
                if top_bit(q) == p:
                    value = value + got[q].astype(F32)
            sent[p] = hop(value.astype(LOW), axis, p)
    return sent


def total(own, *arrived):
    value = own.astype(F32)
    for some in arrived:
        for p in some:
            value = value + some[p].astype(F32)
    return value


def swap_pieces(pieces, axis):
    return {p: hop(pieces[p], axis, p) if p else pieces[p] for p in range(lax.axis_size(axis))}


def stacked(pieces, axis=0):
    return jnp.concatenate([pieces[p] for p in range(len(pieces))], axis=axis)


def relative_blocks(value, axis):
    size = lax.axis_size(axis)
    mine = lax.axis_index(axis)
    step = value.shape[1] // size

    def take(r):
        return lax.dynamic_slice_in_dim(value, (mine ^ r) * step, step, axis=1)

    return (
        jnp.concatenate([take(r) for r in range(0, size, 2)], axis=1),
        jnp.concatenate([take(r) for r in range(1, size, 2)], axis=1),
    )


class DeviceSum:
    def __init__(self, parts, axis):
        self.keep, self.send = [parts[0], parts[2]], [parts[1], parts[3]]
        self.axis, self.turn = axis, 0
        self.flight = None

    def masks(self):
        return 2 << self.turn, (lax.axis_size(self.axis) // 2) >> self.turn

    def land(self):
        self.turn += 1
        for side in (0, 1):
            value = self.keep[side].astype(F32) + self.flight[side].astype(F32)
            half = value.shape[0] // 2
            if half and side == 0:
                self.keep[0], self.send[0] = value[0::2], value[1::2].astype(LOW)
            elif half:
                self.keep[1], self.send[1] = value[:half], value[half:].astype(LOW)
            else:
                self.keep[side] = value

    def result(self):
        return jnp.concatenate([value[0] for value in self.keep], axis=0)

    @property
    def state(self):
        return self.keep, self.send, self.flight

    @state.setter
    def state(self, value):
        self.keep, self.send, self.flight = value


def fly(*sums):
    groups = {}
    for one in sums:
        one.flight = [None, None]
        for side, mask in enumerate(one.masks()):
            groups.setdefault((mask, one.send[side].shape[-1]), []).append((one, side))
    for (mask, wide), parts in sorted(groups.items(), key=lambda item: item[0]):
        rows = [one.send[side].reshape(-1, wide) for one, side in parts]
        flight = hop(jnp.concatenate(rows, axis=0), sums[0].axis, mask)
        start = 0
        for (one, side), some in zip(parts, rows):
            end = start + some.shape[0]
            one.flight[side] = flight[start:end].reshape(one.send[side].shape)
            start = end


def device_steps(axis):
    return (lax.axis_size(axis) // 2).bit_length() - 1


def sum_everywhere(vector, axis):
    bit = 1
    while bit < lax.axis_size(axis):
        vector = vector + hop(vector, axis, bit)
        bit *= 2
    return vector


def rows_by(left, right, contract, precision=None):
    return lax.dot_general(
        left, right, ((contract[:1], contract[1:]), ((), ())), preferred_element_type=F32
    )


def split(value):
    high = value.astype(LOW)
    return high, (value - high.astype(F32)).astype(LOW)


def fine(left, right, contract):
    (lh, ll), (rh, rl) = split(left), split(right)
    return (
        rows_by(lh, rh, contract) + rows_by(lh, rl, contract) + rows_by(ll, rh, contract)
    )


def lifted(values):
    return jnp.where(values > 0, values + 1.0, jnp.exp(jnp.minimum(values, 0.0)))


def lifted_slope(values):
    slope = jnp.exp(jnp.minimum(values, 0.0))
    return jnp.where(values > 0, 1.0, jnp.where(values < 0, slope, 0.5))


def probabilities(queries, key_rows):
    scores = rows_by(queries, key_rows, (1, 1)) * DK ** (-0.5)
    row = lax.broadcasted_iota(jnp.int32, (SEG, SEG), 0)
    col = lax.broadcasted_iota(jnp.int32, (SEG, SEG), 1)
    scores = jnp.where(row >= col, scores, NEGATIVE)
    lift = jnp.exp(scores - jnp.max(scores, axis=-1, keepdims=True))
    return lift / jnp.sum(lift, axis=-1, keepdims=True)


def live_column(segment, length):
    position = segment * SEG + lax.broadcasted_iota(jnp.int32, (SEG, 1), 0)
    return (position < length).astype(F32)


def attend_kernel(place, share, qkv_ref, mixed_ref, memory_ref, normer_ref, memory, normer):
    heads = memory.shape[0]
    width = heads * DK
    segment = pl.program_id(0)

    @pl.when(segment == 0)
    def _():
        memory[...] = jnp.zeros_like(memory)
        normer[...] = jnp.ones_like(normer)

    live = live_column(segment, place[1])
    memory_ref[0] = memory[...]
    normer_ref[0] = normer[...]
    for h in range(heads):
        at = h * DK
        queries = qkv_ref[:, at : at + DK]
        key_rows = qkv_ref[:, width + at : width + at + DK]
        value_rows = qkv_ref[:, 2 * width + at : 2 * width + at + DK]
        probs = probabilities(queries, key_rows).astype(LOW)
        in_block = rows_by(probs, value_rows, (1, 0))
        lifted_q = lifted(queries.astype(F32))
        lifted_k = lifted(key_rows.astype(F32))
        held = memory[h]
        norm = normer[h : h + 1]
        read = fine(jnp.concatenate([lifted_q, lifted_k], axis=0), held, (1, 0))
        recalled = read[:SEG] / jnp.sum(lifted_q * norm, axis=-1, keepdims=True)
        guessed = read[SEG:] / jnp.sum(lifted_k * norm, axis=-1, keepdims=True)
        mix = share[h]
        mixed_ref[:, at : at + DK] = (mix * recalled + (1.0 - mix) * in_block).astype(LOW)
        written = lifted_k * live
        memory[h] = held + fine(written, value_rows.astype(F32) - guessed, (0, 0))
        normer[h : h + 1] = norm + jnp.sum(written, axis=0, keepdims=True)


def attend_back_kernel(
    place, share, qkv_ref, *more_refs
):
    *grad_refs, memory_ref, normer_ref, out_ref, mix_ref, grad_memory, grad_normer, grad_ref = more_refs
    heads = grad_memory.shape[0]
    width = heads * DK
    step = pl.program_id(0)
    segment = pl.num_programs(0) - 1 - step

    @pl.when(step == 0)
    def _():
        grad_memory[...] = jnp.zeros_like(grad_memory)
        grad_normer[...] = jnp.zeros_like(grad_normer)
        mix_ref[...] = jnp.zeros_like(mix_ref)

    per_chunk = pl.num_programs(0) // len(grad_refs)
    chunk = lax.div(segment, per_chunk) ^ place[0]
    start = pl.multiple_of(lax.rem(segment, per_chunk) * SEG, SEG)
    for k, piece_ref in enumerate(grad_refs):

        @pl.when(chunk == k)
        def _():
            grad_ref[...] = piece_ref[pl.ds(start, SEG), :]

    live = live_column(segment, place[1])
    for h in range(heads):
        at = h * DK
        queries = qkv_ref[:, at : at + DK]
        key_rows = qkv_ref[:, width + at : width + at + DK]
        value_rows = qkv_ref[:, 2 * width + at : 2 * width + at + DK]
        grad_mixed = grad_ref[:, at : at + DK].astype(F32)
        mix = share[h]
        probs = probabilities(queries, key_rows)
        probs_low = probs.astype(LOW)
        in_block = rows_by(probs_low, value_rows, (1, 0))
        grad_local = ((1.0 - mix) * grad_mixed).astype(LOW)
        back_v = rows_by(probs_low, grad_local, (0, 0))
        grad_probs = rows_by(grad_local, value_rows, (1, 1))
        inner = jnp.sum(grad_probs * probs, axis=-1, keepdims=True)
        grad_scores = (probs * (grad_probs - inner)).astype(LOW)
        back_q = rows_by(grad_scores, key_rows, (1, 0)) * DK ** (-0.5)
        back_k = rows_by(grad_scores, queries, (0, 0)) * DK ** (-0.5)
        float_q = queries.astype(F32)
        float_k = key_rows.astype(F32)
        lifted_q = lifted(float_q)
        lifted_k = lifted(float_k)
        both = jnp.concatenate([lifted_q, lifted_k], axis=0)
        held = memory_ref[0, h]
        norm = normer_ref[0, h : h + 1]
        over_q = 1.0 / jnp.sum(lifted_q * norm, axis=-1, keepdims=True)
        over_k = 1.0 / jnp.sum(lifted_k * norm, axis=-1, keepdims=True)
        read = fine(both, held, (1, 0))
        recalled = read[:SEG] * over_q
        guessed = read[SEG:] * over_k
        mix_ref[h : h + 1] += jnp.sum(
            grad_mixed * (recalled - in_block), axis=0, keepdims=True
        )
        grad_held = grad_memory[h]
        grad_norm = grad_normer[h : h + 1]
        written = lifted_k * live
        grad_update = fine(written, grad_held, (1, 0))
        grad_written = fine(value_rows.astype(F32) - guessed, grad_held, (1, 1)) + grad_norm
        grad_recalled = mix * grad_mixed
        grad_read_q = grad_recalled * over_q
        grad_read_k = -grad_update * over_k
        grad_sum_q = -jnp.sum(grad_read_q * recalled, axis=-1, keepdims=True)
        grad_sum_k = -jnp.sum(grad_read_k * guessed, axis=-1, keepdims=True)
        grad_reads = jnp.concatenate([grad_read_q, grad_read_k], axis=0)
        back = fine(grad_reads, held, (1, 1))
        grad_lifted_q = back[:SEG] + grad_sum_q * norm
        grad_lifted_k = back[SEG:] + grad_sum_k * norm + live * grad_written
        grad_memory[h] = grad_held + fine(both, grad_reads, (0, 0))
        grad_normer[h : h + 1] = grad_norm + jnp.sum(
            lifted_q * grad_sum_q + lifted_k * grad_sum_k, axis=0, keepdims=True
        )
        out_ref[:, at : at + DK] = (back_q + grad_lifted_q * lifted_slope(float_q)).astype(LOW)
        out_ref[:, width + at : width + at + DK] = (
            back_k + grad_lifted_k * lifted_slope(float_k)
        ).astype(LOW)
        out_ref[:, 2 * width + at : 2 * width + at + DK] = (back_v + grad_update).astype(LOW)


def segment_place(segment, place, per_chunk):
    chunk = lax.div(segment, per_chunk) ^ place[0]
    return chunk * per_chunk + lax.rem(segment, per_chunk)


def attend(qkv, place, share, per_chunk):
    rows, wide = qkv.shape
    heads = wide // (3 * DK)
    blocks = rows // SEG

    def row_map(step, place):
        return (segment_place(step, place, per_chunk), 0)

    return pl.pallas_call(
        attend_kernel,
        name="attend",
        out_shape=(
            jax.ShapeDtypeStruct((rows, heads * DK), LOW),
            jax.ShapeDtypeStruct((blocks, heads, DK, DK), F32),
            jax.ShapeDtypeStruct((blocks, heads, DK), F32),
        ),
        grid_spec=pltpu.PrefetchScalarGridSpec(
            num_scalar_prefetch=1,
            grid=(blocks,),
            in_specs=[
                pl.BlockSpec(memory_space=pltpu.SMEM),
                pl.BlockSpec((SEG, wide), row_map),
            ],
            out_specs=[
                pl.BlockSpec((SEG, heads * DK), row_map),
                pl.BlockSpec((1, heads, DK, DK), lambda step, place: (step, 0, 0, 0)),
                pl.BlockSpec((1, heads, DK), lambda step, place: (step, 0, 0)),
            ],
            scratch_shapes=[pltpu.VMEM((heads, DK, DK), F32), pltpu.VMEM((heads, DK), F32)],
        ),
        compiler_params=pltpu.CompilerParams(
            dimension_semantics=("arbitrary",), vmem_limit_bytes=24 << 20
        ),
        cost_estimate=BRIEF,
    )(place, share, qkv)


def attend_back(qkv, grad_mixed, memories, normers, place, share, per_chunk):
    rows, wide = qkv.shape
    heads = wide // (3 * DK)
    blocks = rows // SEG

    def row_map(step, place):
        return (segment_place(blocks - 1 - step, place, per_chunk), 0)

    return pl.pallas_call(
        attend_back_kernel,
        name="attend_back",
        out_shape=(
            jax.ShapeDtypeStruct((rows, wide), LOW),
            jax.ShapeDtypeStruct((heads, DK), F32),
        ),
        grid_spec=pltpu.PrefetchScalarGridSpec(
            num_scalar_prefetch=1,
            grid=(blocks,),
            in_specs=[
                pl.BlockSpec(memory_space=pltpu.SMEM),
                pl.BlockSpec((SEG, wide), row_map),
                *[whole(piece.shape) for piece in grad_mixed],
                pl.BlockSpec(
                    (1, heads, DK, DK), lambda step, place: (blocks - 1 - step, 0, 0, 0)
                ),
                pl.BlockSpec((1, heads, DK), lambda step, place: (blocks - 1 - step, 0, 0)),
            ],
            out_specs=[
                pl.BlockSpec((SEG, wide), row_map),
                pl.BlockSpec((heads, DK), lambda step, place: (0, 0)),
            ],
            scratch_shapes=[
                pltpu.VMEM((heads, DK, DK), F32),
                pltpu.VMEM((heads, DK), F32),
                pltpu.VMEM((SEG, heads * DK), LOW),
            ],
        ),
        compiler_params=pltpu.CompilerParams(
            dimension_semantics=("arbitrary",), vmem_limit_bytes=24 << 20
        ),
        cost_estimate=pl.CostEstimate(
            flops=blocks * heads * 240 * SEG**3,
            bytes_accessed=rows * wide * 6,
            transcendentals=0,
        ),
    )(place, share, qkv, *grad_mixed, memories, normers)


def live_rows(place, rows):
    position = place[0] * rows + lax.broadcasted_iota(jnp.int32, (rows, 1), 0)
    return (position < place[1]).astype(F32)


def out_project_kernel(place, *refs):
    *mixed_refs, out_ref, tokens_ref, gain_ref, state_ref, normed_ref, beside_ref = refs
    step = pl.program_id(0)

    @pl.when(step == 0)
    def _():
        state_ref[...] = jnp.zeros_like(state_ref)

    weight = out_ref[...].reshape(-1, out_ref.shape[-1])
    for k, mixed_ref in enumerate(mixed_refs):

        @pl.when(step == k)
        def _():
            rows = mixed_ref[...]
            width = rows.shape[1]
            beside_ref[:, k * width : (k + 1) * width] = rows
            state_ref[...] += rows_by(rows, weight, (1, 0))

    @pl.when(step == len(mixed_refs) - 1)
    def _():
        live = live_rows(place, state_ref.shape[0])
        state = tokens_ref[...].astype(F32) + live * state_ref[...]
        state_ref[...] = state
        normed_ref[...] = (state * inverse_rms(state) * gain_ref[...]).astype(LOW)


def out_spec(out_full):
    blocks, _, rows, features = out_full.shape
    return pl.BlockSpec((blocks, 1, rows, features), lambda step, *_: (0, step, 0, 0))


def whole(shape):
    return pl.BlockSpec(shape, lambda *_: (0,) * len(shape))


def out_project(mixed, out_full, tokens, gain, place):
    ranks = len(mixed)
    rows, features = tokens.shape
    width = mixed[0].shape[1]
    return pl.pallas_call(
        out_project_kernel,
        name="out_project",
        out_shape=(
            jax.ShapeDtypeStruct((rows, features), F32),
            jax.ShapeDtypeStruct((rows, features), LOW),
            jax.ShapeDtypeStruct((rows, ranks * width), LOW),
        ),
        grid_spec=pltpu.PrefetchScalarGridSpec(
            num_scalar_prefetch=1,
            grid=(ranks,),
            in_specs=[whole((rows, width))] * ranks
            + [out_spec(out_full), whole((rows, features)), whole((1, features))],
            out_specs=[whole((rows, features))] * 2 + [whole((rows, ranks * width))],
        ),
        compiler_params=pltpu.CompilerParams(
            dimension_semantics=("arbitrary",), vmem_limit_bytes=56 << 20
        ),
        cost_estimate=BRIEF,
    )(place, *[mixed[p] for p in range(ranks)], out_full, tokens, gain[None])


def out_back_kernel(near, place, own_ref, *refs):
    near_refs = refs[:near]
    out_ref, state_ref, up_ref, gain_ref, *refs = refs[near:]
    grad_ref, attn_ref, kept_ref, sent_ref, gain_sum_ref, *back_refs = refs
    step = pl.program_id(0)

    @pl.when(step == 0)
    def _():
        grad = own_ref[...]
        for near_ref in near_refs:
            grad = grad + near_ref[...].astype(F32)
        state = state_ref[...]
        through, gain_sum = normed_back(state, inverse_rms(state), gain_ref[...], grad)
        grad = up_ref[...].astype(F32) + through
        grad_ref[...] = grad
        gain_sum_ref[...] = gain_sum[None]
        attn_ref[...] = (grad * live_rows(place, grad.shape[0])).astype(LOW)
        split_columns(place, attn_ref, kept_ref, sent_ref)

    back = rows_by(attn_ref[...], out_ref[...].reshape(-1, out_ref.shape[-1]), (1, 1)).astype(LOW)
    for k, back_ref in enumerate(back_refs):

        @pl.when(step == k)
        def _():
            back_ref[...] = back


def split_columns(place, source, kept, sent):
    size = lax.axis_size("dp")
    block = source.shape[1] // size
    for r in range(size):
        start = pl.multiple_of((place[2] ^ r) * block, block)
        target = sent if r % 2 else kept
        target[:, r // 2 * block : (r // 2 + 1) * block] = source[:, pl.ds(start, block)]


def out_back(own, near, out_full, state, cotangent, gain, place):
    rows, features = own.shape
    blocks, ranks, slice_rows, _ = out_full.shape
    width = blocks * slice_rows
    square, half = (rows, features), (rows, features // 2)
    shapes = [
        (square, F32), (square, LOW), (half, LOW), (half, LOW), ((1, features), F32),
        *[((rows, width), LOW)] * ranks,
    ]
    grad, _, kept, sent, gain_sum, *backs = pl.pallas_call(
        functools.partial(out_back_kernel, len(near)),
        name="out_back",
        out_shape=[jax.ShapeDtypeStruct(*shape) for shape in shapes],
        grid_spec=pltpu.PrefetchScalarGridSpec(
            num_scalar_prefetch=1,
            grid=(ranks,),
            in_specs=[whole(square)] * (1 + len(near))
            + [out_spec(out_full), whole(square), whole(square), whole((1, features))],
            out_specs=[whole(shape) for shape, _ in shapes],
        ),
        compiler_params=pltpu.CompilerParams(
            dimension_semantics=("arbitrary",), vmem_limit_bytes=56 << 20
        ),
        cost_estimate=BRIEF,
    )(place, own, *near, out_full, state, cotangent, gain[None])
    return grad, kept, sent, gain_sum[0], backs


def feed_kernel(
    place,
    rows_ref,
    branch_ref,
    gate_ref,
    up_ref,
    down_ref,
    made_ref,
    kept_ref,
    sent_ref,
    two_ref,
    mlp_ref,
    two_sum,
    mlp_sum,
):
    step = pl.program_id(0)

    @pl.when(step == 0)
    def _():
        two_sum[...] = jnp.zeros_like(two_sum)
        mlp_sum[...] = jnp.zeros_like(mlp_sum)
        for k, source in enumerate((rows_ref, branch_ref)):
            split_columns(place, source, kept_ref.at[k], sent_ref.at[k])

    rows = rows_ref[...]
    gate_pre = rows_by(rows, gate_ref[...], (1, 0))
    up_pre = rows_by(rows, up_ref[...], (1, 0))
    grad_hidden = rows_by(branch_ref[...], down_ref[...], (1, 1))
    scale, cube = 0.7978845608028654, 0.044715
    square = gate_pre * gate_pre
    bend = jnp.tanh(scale * (gate_pre + cube * (square * gate_pre)))
    half = 0.5 * (1.0 + bend)
    curved = gate_pre * half
    slope = half + (0.5 * scale) * gate_pre * (1.0 - bend * bend) * (1.0 + (3.0 * cube) * square)
    hidden = (curved * up_pre).astype(LOW)
    gate_back = (grad_hidden * up_pre * slope).astype(LOW)
    up_back = (grad_hidden * curved).astype(LOW)
    made_ref[0] = hidden
    made_ref[1] = gate_back
    made_ref[2] = up_back
    two_sum[...] += rows_by(gate_back, gate_ref[...], (1, 1)) + rows_by(up_back, up_ref[...], (1, 1))
    mlp_sum[...] += rows_by(hidden, down_ref[...], (1, 0))

    @pl.when(step == pl.num_programs(0) - 1)
    def _():
        two_ref[...] = two_sum[...].astype(two_ref.dtype)
        mlp_ref[...] = mlp_sum[...].astype(mlp_ref.dtype)


def feed_forward(rows, branch, gate_weight, up_weight, down_weight, place, kind):
    count, features = rows.shape
    units = gate_weight.shape[1]
    tile = min(512, units)
    columns = pl.BlockSpec((features, tile), lambda step, place: (0, step))
    half = (2, count, features // 2)
    return pl.pallas_call(
        feed_kernel,
        name="feed_forward",
        out_shape=(
            jax.ShapeDtypeStruct((3, count, units), LOW),
            *[jax.ShapeDtypeStruct(half, LOW)] * 2,
            *[jax.ShapeDtypeStruct((count, features), kind)] * 2,
        ),
        grid_spec=pltpu.PrefetchScalarGridSpec(
            num_scalar_prefetch=1,
            grid=(units // tile,),
            in_specs=[
                whole((count, features)),
                whole((count, features)),
                columns,
                columns,
                pl.BlockSpec((tile, features), lambda step, place: (step, 0)),
            ],
            out_specs=[
                pl.BlockSpec((3, count, tile), lambda step, place: (0, 0, step)),
                *[whole(half)] * 2,
                *[whole((count, features))] * 2,
            ],
            scratch_shapes=[pltpu.VMEM((count, features), F32)] * 2,
        ),
        compiler_params=pltpu.CompilerParams(
            dimension_semantics=("arbitrary",), vmem_limit_bytes=44 << 20
        ),
        cost_estimate=BRIEF,
    )(place, rows, branch, gate_weight, up_weight, down_weight)


def project_back_kernel(*refs):
    count = (len(refs) - 2) // 3
    rows_refs, one_refs, weight_ref = refs[:count], refs[count : 2 * count], refs[2 * count]
    out_refs, gain_ref = refs[2 * count + 1 : -1], refs[-1]
    weight = weight_ref[...]
    gain = jnp.zeros(gain_ref.shape, F32)
    for rows_ref, one_ref, out_ref in zip(rows_refs, one_refs, out_refs):
        value = rows_by(rows_ref[...], weight, (1, 1))
        out_ref[...] = value.astype(out_ref.dtype)
        gain = gain + jnp.sum(value * one_ref[...].astype(F32), axis=0, keepdims=True)
    gain_ref[...] = gain


def project_rows_back(rows, weight, count, one, wanted, kinds):
    features, wide = weight.shape
    tile = min(512, features)
    made = pl.BlockSpec((count, tile), lambda step: (0, step))
    *parts, gain = pl.pallas_call(
        project_back_kernel,
        name="project_back",
        out_shape=[jax.ShapeDtypeStruct((count, features), kind) for kind in kinds]
        + [jax.ShapeDtypeStruct((1, features), F32)],
        grid=(features // tile,),
        in_specs=[pl.BlockSpec((count, wide), lambda step, p=p: (p, 0)) for p in wanted]
        + [made] * len(wanted)
        + [pl.BlockSpec((tile, wide), lambda step: (step, 0))],
        out_specs=[made] * len(wanted) + [pl.BlockSpec((1, tile), lambda step: (0, step))],
        compiler_params=pltpu.CompilerParams(
            dimension_semantics=("arbitrary",), vmem_limit_bytes=24 << 20
        ),
        cost_estimate=BRIEF,
    )(*[rows] * len(wanted), *[one[p] for p in wanted], weight)
    return dict(zip(wanted, parts)), gain[0]


def weight_kernel(*refs):
    *in_refs, low_keep, low_send, high_keep, high_send = refs
    half = len(in_refs) // 2
    step = pl.program_id(0)
    steps = pl.num_programs(0)
    value = rows_by(in_refs[0][...], in_refs[half][...], (0, 0))
    for left, right in zip(in_refs[1:half], in_refs[half + 1 :]):
        value = value + rows_by(left[...], right[...], (0, 0))
    value = value.astype(LOW)
    middle = value.shape[0] // 2
    odd = lax.rem(step, 2) == 1
    upper = step >= steps // 2

    @pl.when(jnp.logical_not(odd))
    def _():
        low_keep[...] = value[:middle]

    @pl.when(odd)
    def _():
        low_send[...] = value[:middle]

    @pl.when(jnp.logical_not(upper))
    def _():
        high_keep[...] = value[middle:]

    @pl.when(upper)
    def _():
        high_send[...] = value[middle:]


def weight_blocks(lefts, rights, blocks):
    across = lefts[0][0].shape[2] // blocks
    along = rights[0][0].shape[2]

    def left_spec(pair):
        return pl.BlockSpec((None, pair[0].shape[1], across), lambda step: (pair[1], 0, step))

    def right_spec(pair):
        return pl.BlockSpec((None, pair[0].shape[1], along), lambda step: (pair[1], 0, 0))

    def out_spec_of(place):
        return pl.BlockSpec((None, across // 2, along), lambda step: (place(step), 0, 0))

    half = blocks // 2
    return pl.pallas_call(
        weight_kernel,
        name="weight_blocks",
        out_shape=[jax.ShapeDtypeStruct((half, across // 2, along), LOW)] * 4,
        grid=(blocks,),
        in_specs=[left_spec(pair) for pair in lefts] + [right_spec(pair) for pair in rights],
        out_specs=[
            out_spec_of(lambda step: lax.div(step, 2)),
            out_spec_of(lambda step: lax.div(step, 2)),
            out_spec_of(lambda step: jnp.minimum(step, half - 1)),
            out_spec_of(lambda step: jnp.maximum(step - half, 0)),
        ],
        compiler_params=pltpu.CompilerParams(
            dimension_semantics=("arbitrary",), vmem_limit_bytes=40 << 20
        ),
        cost_estimate=BRIEF,
    )(*[pair[0] for pair in lefts], *[pair[0] for pair in rights])


def inverse_rms(values):
    return lax.rsqrt(jnp.mean(values * values, axis=-1, keepdims=True) + EPS)


def normed_back(values, inverse, gain_vec, grad):
    unit = values * inverse
    scaled = grad * gain_vec
    grad_values = inverse * (scaled - unit * jnp.mean(scaled * unit, axis=-1, keepdims=True))
    return grad_values, jnp.sum(grad * unit, axis=0)


def hold(value):
    return lax.optimization_barrier(value)


def shards(
    tokens,
    cotangent,
    lengths,
    query_weight,
    key_weight,
    value_weight,
    out_weight,
    gate_weight,
    up_weight,
    down_weight,
    attn_gain,
    mlp_gain,
    memory_gate,
):
    ranks = lax.axis_size("mp")
    row_count = tokens.shape[0]
    width = query_weight.shape[1]
    heads = width // DK
    per_chunk = row_count // SEG
    rank = lax.axis_index("mp")
    pieces = range(ranks)
    place = jnp.stack([rank, lengths[0], lax.axis_index("dp")]).astype(jnp.int32)
    live = (rank * row_count + jnp.arange(row_count) < lengths[0]).astype(F32)[:, None]
    share = jax.nn.sigmoid(memory_gate)

    features = tokens.shape[1]
    blocks = lax.axis_size("dp")
    near, far = singles(ranks), doubles(ranks)

    def product(left, right):
        return rows_by(left, right, (0, 0)).astype(LOW)

    inputs = tokens.astype(F32)
    inverse_one = inverse_rms(inputs)
    normed_one = (inputs * inverse_one * attn_gain).astype(LOW)
    slice_rows = width // blocks
    out_slice = lax.dynamic_slice_in_dim(
        out_weight, lax.axis_index("dp") * slice_rows, slice_rows, axis=0
    )
    out_slice, normed_one = hold((out_slice, normed_one))
    qkv_weight = jnp.concatenate([query_weight, key_weight, value_weight], axis=1)

    def project(rows):
        return rows_by(rows, qkv_weight, (1, 0)).astype(LOW)

    one = gather_near(normed_one, "mp")
    out_slices = gather_near(out_slice, "mp")
    qkv = {0: project(one[0])}
    one, out_slices, qkv, qkv_weight = hold((one, out_slices, qkv, qkv_weight))

    one.update(gather_far(one, "mp"))
    out_slices.update(gather_far(out_slices, "mp"))
    qkv.update({p: project(one[p]) for p in near})
    upstream = cotangent.astype(F32)
    branch_mine = (upstream * live).astype(LOW)
    one, out_slices, qkv, branch_mine = hold((one, out_slices, qkv, branch_mine))
    out_full = lax.all_gather(
        jnp.stack([out_slices[p] for p in pieces]), "dp", axis=0, tiled=True
    )

    branch = gather_near(branch_mine, "mp")
    qkv.update({p: project(one[p]) for p in far})
    qkv = stacked(qkv)
    mixed, memories, normers = attend(qkv, place, share, per_chunk)
    mixed = hold(mixed)

    mixed = swap_pieces(
        {p: mixed[p * row_count : (p + 1) * row_count] for p in pieces}, "mp"
    )
    mixed, branch = hold((mixed, branch))

    out_full = out_full.reshape(blocks, ranks, slice_rows, features)
    state, normed_two, mixed = out_project(mixed, out_full, tokens, mlp_gain, place)

    made, kept, sent, two_parts, mlp_parts = {}, {}, {}, {}, {}

    def feed(p):
        kind = LOW if p == 1 or p in far else F32
        made[p], kept[p], sent[p], two_parts[p], mlp_parts[p] = feed_forward(
            two[p], branch[p], gate_weight, up_weight, down_weight, place, kind
        )

    their_made, their_kept = {}, {}

    def share_rows(p):
        their_made[p] = hop(made[p], "dp", 1)
        their_kept[p] = hop(sent[p], "dp", 1)

    two = gather_near(normed_two, "mp")
    branch.update(gather_far(branch, "mp"))
    feed(0)
    one_kept, one_sent = relative_blocks(stacked(one), "dp")
    their_mixed = hop(mixed, "dp", 1)
    two, made, kept, sent, two_parts, mlp_parts, branch, one_kept, one_sent, their_mixed = hold(
        (two, made, kept, sent, two_parts, mlp_parts, branch, one_kept, one_sent, their_mixed)
    )

    two.update(gather_far(two, "mp"))
    share_rows(0)
    their_one = hop(one_sent, "dp", 1)
    feed(1)
    two, made, kept, sent, two_parts, mlp_parts, their_made, their_kept, their_one = hold(
        (two, made, kept, sent, two_parts, mlp_parts, their_made, their_kept, their_one)
    )

    mlp_near = reduce_near(mlp_parts, None, "mp", (1,))
    share_rows(1)
    for p in far:
        feed(p)
    two, made, kept, sent, two_parts, mlp_parts, their_made, their_kept, mlp_near = hold(
        (two, made, kept, sent, two_parts, mlp_parts, their_made, their_kept, mlp_near)
    )

    two_far = reduce_far(two_parts, "mp")
    for p in far:
        share_rows(p)
    for p in near[1:]:
        feed(p)
    made, kept, sent, two_parts, mlp_parts, their_made, their_kept, two_far = hold(
        (made, kept, sent, two_parts, mlp_parts, their_made, their_kept, two_far)
    )

    steps = device_steps("dp")

    def weights_of(left, right):
        return DeviceSum(
            weight_blocks(
                [(kept[p], left) for p in pieces] + [(their_kept[p], left) for p in pieces],
                [(made[p], right) for p in pieces] + [(their_made[p], right) for p in pieces],
                blocks // 2,
            ),
            "dp",
        )

    two_near = reduce_near(two_parts, two_far, "mp")
    for p in near[1:]:
        share_rows(p)
    gate_sum = weights_of(0, 1)
    fly(gate_sum)
    up_sum = weights_of(0, 2)
    down_sum = weights_of(1, 0)
    two_near, mlp_parts, gate_sum.state, up_sum.state, down_sum.state = hold(
        (two_near, mlp_parts, gate_sum.state, up_sum.state, down_sum.state)
    )

    mlp_far = reduce_far(mlp_parts, "mp")
    fly(up_sum)
    grad_state, attn_kept, attn_sent, grad_mlp_gain, grad_mixed = out_back(
        two_parts[0],
        [two_near[p] for p in sorted(two_near)],
        out_full,
        state,
        cotangent,
        mlp_gain,
        place,
    )
    their_attn = hop(attn_sent, "dp", 1)
    (
        mlp_far, grad_mixed, attn_kept, their_attn, grad_state, grad_mlp_gain, mlp_parts,
        gate_sum.state, up_sum.state, down_sum.state,
    ) = hold(
        (
            mlp_far, grad_mixed, attn_kept, their_attn, grad_state, grad_mlp_gain, mlp_parts,
            gate_sum.state, up_sum.state, down_sum.state,
        )
    )
    grad_mixed = swap_pieces(grad_mixed, "mp")
    fly(down_sum)
    out_sum = DeviceSum(
        weight_blocks(
            [(attn_kept[None], 0), (their_attn[None], 0)],
            [(mixed[None], 0), (their_mixed[None], 0)],
            blocks // 2,
        ),
        "dp",
    )
    gate_sum.land()
    up_sum.land()
    grad_mixed, mlp_parts, gate_sum.state, up_sum.state, down_sum.state, out_sum.state = hold(
        (grad_mixed, mlp_parts, gate_sum.state, up_sum.state, down_sum.state, out_sum.state)
    )

    mlp_near.update(reduce_near(mlp_parts, mlp_far, "mp", near[1:]))
    fly(out_sum, *([gate_sum, up_sum] if steps > 1 else []))
    down_sum.land()
    grad_qkv, grad_mix = attend_back(
        qkv, [grad_mixed[p] for p in pieces], memories, normers, place, share, per_chunk
    )
    grad_qkv, grad_mix, mlp_near, out_sum.state, down_sum.state, gate_sum.state, up_sum.state = hold(
        (grad_qkv, grad_mix, mlp_near, out_sum.state, down_sum.state, gate_sum.state, up_sum.state)
    )

    def project_back(wanted):
        kinds = [LOW if p == 1 or p in far else F32 for p in wanted]
        return project_rows_back(grad_qkv, qkv_weight, row_count, one, wanted, kinds)

    their_qkv = hop(grad_qkv, "dp", 1)
    one_parts, gain_far = project_back(far)
    one_parts, grad_qkv, out_sum.state, down_sum.state, mlp_near = hold(
        (one_parts, grad_qkv, out_sum.state, down_sum.state, mlp_near)
    )
    one_far = reduce_far(one_parts, "mp")
    qkv_sum = DeviceSum(
        weight_blocks(
            [(one_kept[None], 0), (their_one[None], 0)],
            [(grad_qkv[None], 0), (their_qkv[None], 0)],
            blocks // 2,
        ),
        "dp",
    )
    grad_qkv, qkv_sum.state, out_sum.state, down_sum.state = hold(
        (grad_qkv, qkv_sum.state, out_sum.state, down_sum.state)
    )
    out_sum.land()
    if steps > 1:
        fly(down_sum, out_sum)
    more_parts, gain_near = project_back([0] + near)
    one_parts.update(more_parts)
    one_parts, one_far, qkv_sum.state, mlp_near = hold(
        (one_parts, one_far, qkv_sum.state, mlp_near)
    )

    one_near = reduce_near(one_parts, one_far, "mp")
    block_out = (state + live * total(mlp_parts[0], mlp_near)).astype(LOW)
    grad_attn_gain = (gain_far + gain_near) / attn_gain
    grad_share = jnp.sum(grad_mix, axis=1) * share * (1.0 - share)
    share_full = lax.dynamic_update_slice(
        jnp.zeros((heads * ranks,), F32), grad_share, (rank * heads,)
    )
    small = jnp.concatenate([grad_attn_gain, grad_mlp_gain, share_full])
    fly(qkv_sum)
    for k in range(1, steps):
        for some in ([gate_sum, up_sum], [down_sum, out_sum]):
            for one_sum in some:
                one_sum.land()
            if k + 1 < steps:
                fly(*some)
        qkv_sum.land()
        fly(qkv_sum)
    qkv_sum.land()
    grad_gate, grad_up = gate_sum.result(), up_sum.result()
    grad_down = down_sum.result().T
    grad_proj = qkv_sum.result()
    grad_out_part = out_sum.result()
    out_parts = {p: grad_out_part[:, p * width : (p + 1) * width] for p in pieces}
    out_parts = {p: out_parts[p].astype(LOW) if p else out_parts[p] for p in pieces}
    one_near, small, out_parts, block_out, grad_gate, grad_up, grad_down, grad_proj = hold(
        (one_near, small, out_parts, block_out, grad_gate, grad_up, grad_down, grad_proj)
    )

    small = sum_everywhere(sum_everywhere(small, "mp"), "dp")
    grad_out = total(
        out_parts[0], {p: hop(out_parts[p], "mp", p) for p in range(1, ranks)}
    ).T
    grad_query, grad_key, grad_value = (
        grad_proj[:, j * width : (j + 1) * width] for j in range(3)
    )
    grad_normed_one = total(one_parts[0], one_near)
    grad_inputs = normed_back(inputs, inverse_one, attn_gain, grad_normed_one)[0]
    grad_tokens = grad_state + grad_inputs
    return (
        block_out,
        grad_tokens,
        grad_query,
        grad_key,
        grad_value,
        grad_out,
        grad_gate,
        grad_up,
        grad_down,
        small[:features],
        small[features : 2 * features],
        small[2 * features : 2 * features + heads * ranks],
    )


def solution(mesh):
    return jax.shard_map(
        shards,
        mesh=mesh,
        in_specs=(
            P(("dp", "mp"), None),
            P(("dp", "mp"), None),
            P("dp"),
            P(None, "mp"),
            P(None, "mp"),
            P(None, "mp"),
            P("mp", None),
            P(None, "mp"),
            P(None, "mp"),
            P("mp", None),
            P(),
            P(),
            P("mp"),
        ),
        out_specs=(
            P(("dp", "mp"), None),
            P(("dp", "mp"), None),
            P("dp", "mp"),
            P("dp", "mp"),
            P("dp", "mp"),
            P("mp", "dp"),
            P("dp", "mp"),
            P("dp", "mp"),
            P("mp", "dp"),
            P(),
            P(),
            P(),
        ),
        check_vma=False,
    )
```

```python
import functools

import jax
import jax.numpy as jnp
from jax import lax
from jax.experimental import pallas as pl
from jax.experimental.pallas import tpu as pltpu
from jax.sharding import PartitionSpec as P

DK = 128
SEG = 128
EPS = 1e-05
NEGATIVE = -1e30
LOW = jnp.bfloat16
F32 = jnp.float32
BRIEF = pl.CostEstimate(flops=1, bytes_accessed=1, transcendentals=0)


def hop(value, axis, mask):
    size = lax.axis_size(axis)
    return lax.ppermute(value, axis, [(j, j ^ mask) for j in range(size)])


def top_bit(number):
    return 1 << (number.bit_length() - 1)


def singles(size):
    return [p for p in range(1, size) if p == top_bit(p)]


def doubles(size):
    return [p for p in range(1, size) if p != top_bit(p)]


def gather_near(mine, axis):
    return {0: mine, **{p: hop(mine, axis, p) for p in singles(lax.axis_size(axis))}}


def gather_far(pieces, axis):
    size = lax.axis_size(axis)
    return {p: hop(pieces[top_bit(p)], axis, p ^ top_bit(p)) for p in doubles(size)}


def reduce_far(parts, axis):
    size = lax.axis_size(axis)
    return {p: hop(parts[p].astype(LOW), axis, p ^ top_bit(p)) for p in doubles(size)}


def reduce_near(parts, got, axis, only=None):
    size = lax.axis_size(axis)
    sent = {}
    for p in singles(size):
        if only is None or p in only:
            value = parts[p].astype(F32)
            for q in doubles(size):
                if top_bit(q) == p:
                    value = value + got[q].astype(F32)
            sent[p] = hop(value.astype(LOW), axis, p)
    return sent


def total(own, *arrived):
    value = own.astype(F32)
    for some in arrived:
        for p in some:
            value = value + some[p].astype(F32)
    return value


def swap_pieces(pieces, axis):
    return {p: hop(pieces[p], axis, p) if p else pieces[p] for p in range(lax.axis_size(axis))}


def stacked(pieces, axis=0):
    return jnp.concatenate([pieces[p] for p in range(len(pieces))], axis=axis)


def relative_blocks(value, axis):
    size = lax.axis_size(axis)
    mine = lax.axis_index(axis)
    step = value.shape[1] // size

    def take(r):
        return lax.dynamic_slice_in_dim(value, (mine ^ r) * step, step, axis=1)

    return (
        jnp.concatenate([take(r) for r in range(0, size, 2)], axis=1),
        jnp.concatenate([take(r) for r in range(1, size, 2)], axis=1),
    )


class DeviceSum:
    def __init__(self, parts, axis):
        self.keep, self.send = [parts[0], parts[2]], [parts[1], parts[3]]
        self.axis, self.turn = axis, 0
        self.flight = None

    def masks(self):
        return 2 << self.turn, (lax.axis_size(self.axis) // 2) >> self.turn

    def land(self):
        self.turn += 1
        for side in (0, 1):
            value = self.keep[side].astype(F32) + self.flight[side].astype(F32)
            half = value.shape[0] // 2
            if half and side == 0:
                self.keep[0], self.send[0] = value[0::2], value[1::2].astype(LOW)
            elif half:
                self.keep[1], self.send[1] = value[:half], value[half:].astype(LOW)
            else:
                self.keep[side] = value

    def result(self):
        return jnp.concatenate([value[0] for value in self.keep], axis=0)

    @property
    def state(self):
        return self.keep, self.send, self.flight

    @state.setter
    def state(self, value):
        self.keep, self.send, self.flight = value


def fly(*sums):
    groups = {}
    for one in sums:
        one.flight = [None, None]
        for side, mask in enumerate(one.masks()):
            groups.setdefault((mask, one.send[side].shape[-1]), []).append((one, side))
    for (mask, wide), parts in sorted(groups.items(), key=lambda item: item[0]):
        rows = [one.send[side].reshape(-1, wide) for one, side in parts]
        flight = hop(jnp.concatenate(rows, axis=0), sums[0].axis, mask)
        start = 0
        for (one, side), some in zip(parts, rows):
            end = start + some.shape[0]
            one.flight[side] = flight[start:end].reshape(one.send[side].shape)
            start = end


def device_steps(axis):
    return (lax.axis_size(axis) // 2).bit_length() - 1


def sum_everywhere(vector, axis):
    bit = 1
    while bit < lax.axis_size(axis):
        vector = vector + hop(vector, axis, bit)
        bit *= 2
    return vector


def rows_by(left, right, contract, precision=None):
    return lax.dot_general(
        left, right, ((contract[:1], contract[1:]), ((), ())), preferred_element_type=F32
    )


def split(value):
    high = value.astype(LOW)
    return high, (value - high.astype(F32)).astype(LOW)


def fine(left, right, contract):
    (lh, ll), (rh, rl) = split(left), split(right)
    return (
        rows_by(lh, rh, contract) + rows_by(lh, rl, contract) + rows_by(ll, rh, contract)
    )


def lifted(values):
    return jnp.where(values > 0, values + 1.0, jnp.exp(jnp.minimum(values, 0.0)))


def lifted_slope(values):
    slope = jnp.exp(jnp.minimum(values, 0.0))
    return jnp.where(values > 0, 1.0, jnp.where(values < 0, slope, 0.5))


def probabilities(queries, key_rows):
    scores = rows_by(queries, key_rows, (1, 1)) * DK ** (-0.5)
    row = lax.broadcasted_iota(jnp.int32, (SEG, SEG), 0)
    col = lax.broadcasted_iota(jnp.int32, (SEG, SEG), 1)
    scores = jnp.where(row >= col, scores, NEGATIVE)
    lift = jnp.exp(scores - jnp.max(scores, axis=-1, keepdims=True))
    return lift / jnp.sum(lift, axis=-1, keepdims=True)


def live_column(segment, length):
    position = segment * SEG + lax.broadcasted_iota(jnp.int32, (SEG, 1), 0)
    return (position < length).astype(F32)


def attend_kernel(place, share, qkv_ref, mixed_ref, memory_ref, normer_ref, memory, normer):
    heads = memory.shape[0]
    width = heads * DK
    segment = pl.program_id(0)

    @pl.when(segment == 0)
    def _():
        memory[...] = jnp.zeros_like(memory)
        normer[...] = jnp.ones_like(normer)

    live = live_column(segment, place[1])
    memory_ref[0] = memory[...]
    normer_ref[0] = normer[...]
    for h in range(heads):
        at = h * DK
        queries = qkv_ref[:, at : at + DK]
        key_rows = qkv_ref[:, width + at : width + at + DK]
        value_rows = qkv_ref[:, 2 * width + at : 2 * width + at + DK]
        probs = probabilities(queries, key_rows).astype(LOW)
        in_block = rows_by(probs, value_rows, (1, 0))
        lifted_q = lifted(queries.astype(F32))
        lifted_k = lifted(key_rows.astype(F32))
        held = memory[h]
        norm = normer[h : h + 1]
        read = fine(jnp.concatenate([lifted_q, lifted_k], axis=0), held, (1, 0))
        recalled = read[:SEG] / jnp.sum(lifted_q * norm, axis=-1, keepdims=True)
        guessed = read[SEG:] / jnp.sum(lifted_k * norm, axis=-1, keepdims=True)
        mix = share[h]
        mixed_ref[:, at : at + DK] = (mix * recalled + (1.0 - mix) * in_block).astype(LOW)
        written = lifted_k * live
        memory[h] = held + fine(written, value_rows.astype(F32) - guessed, (0, 0))
        normer[h : h + 1] = norm + jnp.sum(written, axis=0, keepdims=True)


def attend_back_kernel(
    place, share, qkv_ref, *more_refs
):
    *grad_refs, memory_ref, normer_ref, out_ref, mix_ref, grad_memory, grad_normer, grad_ref = more_refs
    heads = grad_memory.shape[0]
    width = heads * DK
    step = pl.program_id(0)
    segment = pl.num_programs(0) - 1 - step

    @pl.when(step == 0)
    def _():
        grad_memory[...] = jnp.zeros_like(grad_memory)
        grad_normer[...] = jnp.zeros_like(grad_normer)
        mix_ref[...] = jnp.zeros_like(mix_ref)

    per_chunk = pl.num_programs(0) // len(grad_refs)
    chunk = lax.div(segment, per_chunk) ^ place[0]
    start = pl.multiple_of(lax.rem(segment, per_chunk) * SEG, SEG)
    for k, piece_ref in enumerate(grad_refs):

        @pl.when(chunk == k)
        def _():
            grad_ref[...] = piece_ref[pl.ds(start, SEG), :]

    live = live_column(segment, place[1])
    for h in range(heads):
        at = h * DK
        queries = qkv_ref[:, at : at + DK]
        key_rows = qkv_ref[:, width + at : width + at + DK]
        value_rows = qkv_ref[:, 2 * width + at : 2 * width + at + DK]
        grad_mixed = grad_ref[:, at : at + DK].astype(F32)
        mix = share[h]
        probs = probabilities(queries, key_rows)
        probs_low = probs.astype(LOW)
        in_block = rows_by(probs_low, value_rows, (1, 0))
        grad_local = ((1.0 - mix) * grad_mixed).astype(LOW)
        back_v = rows_by(probs_low, grad_local, (0, 0))
        grad_probs = rows_by(grad_local, value_rows, (1, 1))
        inner = jnp.sum(grad_probs * probs, axis=-1, keepdims=True)
        grad_scores = (probs * (grad_probs - inner)).astype(LOW)
        back_q = rows_by(grad_scores, key_rows, (1, 0)) * DK ** (-0.5)
        back_k = rows_by(grad_scores, queries, (0, 0)) * DK ** (-0.5)
        float_q = queries.astype(F32)
        float_k = key_rows.astype(F32)
        lifted_q = lifted(float_q)
        lifted_k = lifted(float_k)
        both = jnp.concatenate([lifted_q, lifted_k], axis=0)
        held = memory_ref[0, h]
        norm = normer_ref[0, h : h + 1]
        over_q = 1.0 / jnp.sum(lifted_q * norm, axis=-1, keepdims=True)
        over_k = 1.0 / jnp.sum(lifted_k * norm, axis=-1, keepdims=True)
        read = fine(both, held, (1, 0))
        recalled = read[:SEG] * over_q
        guessed = read[SEG:] * over_k
        mix_ref[h : h + 1] += jnp.sum(
            grad_mixed * (recalled - in_block), axis=0, keepdims=True
        )
        grad_held = grad_memory[h]
        grad_norm = grad_normer[h : h + 1]
        written = lifted_k * live
        grad_update = fine(written, grad_held, (1, 0))
        grad_written = fine(value_rows.astype(F32) - guessed, grad_held, (1, 1)) + grad_norm
        grad_recalled = mix * grad_mixed
        grad_read_q = grad_recalled * over_q
        grad_read_k = -grad_update * over_k
        grad_sum_q = -jnp.sum(grad_read_q * recalled, axis=-1, keepdims=True)
        grad_sum_k = -jnp.sum(grad_read_k * guessed, axis=-1, keepdims=True)
        grad_reads = jnp.concatenate([grad_read_q, grad_read_k], axis=0)
        back = fine(grad_reads, held, (1, 1))
        grad_lifted_q = back[:SEG] + grad_sum_q * norm
        grad_lifted_k = back[SEG:] + grad_sum_k * norm + live * grad_written
        grad_memory[h] = grad_held + fine(both, grad_reads, (0, 0))
        grad_normer[h : h + 1] = grad_norm + jnp.sum(
            lifted_q * grad_sum_q + lifted_k * grad_sum_k, axis=0, keepdims=True
        )
        out_ref[:, at : at + DK] = (back_q + grad_lifted_q * lifted_slope(float_q)).astype(LOW)
        out_ref[:, width + at : width + at + DK] = (
            back_k + grad_lifted_k * lifted_slope(float_k)
        ).astype(LOW)
        out_ref[:, 2 * width + at : 2 * width + at + DK] = (back_v + grad_update).astype(LOW)


def segment_place(segment, place, per_chunk):
    chunk = lax.div(segment, per_chunk) ^ place[0]
    return chunk * per_chunk + lax.rem(segment, per_chunk)


def attend(qkv, place, share, per_chunk):
    rows, wide = qkv.shape
    heads = wide // (3 * DK)
    blocks = rows // SEG

    def row_map(step, place):
        return (segment_place(step, place, per_chunk), 0)

    return pl.pallas_call(
        attend_kernel,
        name="attend",
        out_shape=(
            jax.ShapeDtypeStruct((rows, heads * DK), LOW),
            jax.ShapeDtypeStruct((blocks, heads, DK, DK), F32),
            jax.ShapeDtypeStruct((blocks, heads, DK), F32),
        ),
        grid_spec=pltpu.PrefetchScalarGridSpec(
            num_scalar_prefetch=1,
            grid=(blocks,),
            in_specs=[
                pl.BlockSpec(memory_space=pltpu.SMEM),
                pl.BlockSpec((SEG, wide), row_map),
            ],
            out_specs=[
                pl.BlockSpec((SEG, heads * DK), row_map),
                pl.BlockSpec((1, heads, DK, DK), lambda step, place: (step, 0, 0, 0)),
                pl.BlockSpec((1, heads, DK), lambda step, place: (step, 0, 0)),
            ],
            scratch_shapes=[pltpu.VMEM((heads, DK, DK), F32), pltpu.VMEM((heads, DK), F32)],
        ),
        compiler_params=pltpu.CompilerParams(
            dimension_semantics=("arbitrary",), vmem_limit_bytes=24 << 20
        ),
        cost_estimate=BRIEF,
    )(place, share, qkv)


def attend_back(qkv, grad_mixed, memories, normers, place, share, per_chunk):
    rows, wide = qkv.shape
    heads = wide // (3 * DK)
    blocks = rows // SEG

    def row_map(step, place):
        return (segment_place(blocks - 1 - step, place, per_chunk), 0)

    return pl.pallas_call(
        attend_back_kernel,
        name="attend_back",
        out_shape=(
            jax.ShapeDtypeStruct((rows, wide), LOW),
            jax.ShapeDtypeStruct((heads, DK), F32),
        ),
        grid_spec=pltpu.PrefetchScalarGridSpec(
            num_scalar_prefetch=1,
            grid=(blocks,),
            in_specs=[
                pl.BlockSpec(memory_space=pltpu.SMEM),
                pl.BlockSpec((SEG, wide), row_map),
                *[whole(piece.shape) for piece in grad_mixed],
                pl.BlockSpec(
                    (1, heads, DK, DK), lambda step, place: (blocks - 1 - step, 0, 0, 0)
                ),
                pl.BlockSpec((1, heads, DK), lambda step, place: (blocks - 1 - step, 0, 0)),
            ],
            out_specs=[
                pl.BlockSpec((SEG, wide), row_map),
                pl.BlockSpec((heads, DK), lambda step, place: (0, 0)),
            ],
            scratch_shapes=[
                pltpu.VMEM((heads, DK, DK), F32),
                pltpu.VMEM((heads, DK), F32),
                pltpu.VMEM((SEG, heads * DK), LOW),
            ],
        ),
        compiler_params=pltpu.CompilerParams(
            dimension_semantics=("arbitrary",), vmem_limit_bytes=24 << 20
        ),
        cost_estimate=pl.CostEstimate(
            flops=blocks * heads * 240 * SEG**3,
            bytes_accessed=rows * wide * 6,
            transcendentals=0,
        ),
    )(place, share, qkv, *grad_mixed, memories, normers)


def live_rows(place, rows):
    position = place[0] * rows + lax.broadcasted_iota(jnp.int32, (rows, 1), 0)
    return (position < place[1]).astype(F32)


def out_project_kernel(place, *refs):
    *mixed_refs, out_ref, tokens_ref, gain_ref, state_ref, normed_ref, beside_ref, piece = refs
    step = pl.program_id(0)

    @pl.when(step == 0)
    def _():
        state_ref[...] = jnp.zeros_like(state_ref)

    weight = out_ref[...].reshape(-1, out_ref.shape[-1])
    for k, mixed_ref in enumerate(mixed_refs):

        @pl.when(step == k)
        def _():
            rows = mixed_ref[...]
            width = rows.shape[1]
            beside_ref[:, k * width : (k + 1) * width] = rows
            piece[...] = rows

    state_ref[...] += rows_by(piece[...], weight, (1, 0))

    @pl.when(step == len(mixed_refs) - 1)
    def _():
        live = live_rows(place, state_ref.shape[0])
        state = tokens_ref[...].astype(F32) + live * state_ref[...]
        state_ref[...] = state
        normed_ref[...] = (state * inverse_rms(state) * gain_ref[...]).astype(LOW)


def out_spec(out_full):
    blocks, _, rows, features = out_full.shape
    return pl.BlockSpec((blocks, 1, rows, features), lambda step, *_: (0, step, 0, 0))


def whole(shape):
    return pl.BlockSpec(shape, lambda *_: (0,) * len(shape))


def out_project(mixed, out_full, tokens, gain, place):
    ranks = len(mixed)
    rows, features = tokens.shape
    width = mixed[0].shape[1]
    return pl.pallas_call(
        out_project_kernel,
        name="out_project",
        out_shape=(
            jax.ShapeDtypeStruct((rows, features), F32),
            jax.ShapeDtypeStruct((rows, features), LOW),
            jax.ShapeDtypeStruct((rows, ranks * width), LOW),
        ),
        grid_spec=pltpu.PrefetchScalarGridSpec(
            num_scalar_prefetch=1,
            grid=(ranks,),
            in_specs=[whole((rows, width))] * ranks
            + [out_spec(out_full), whole((rows, features)), whole((1, features))],
            out_specs=[whole((rows, features))] * 2 + [whole((rows, ranks * width))],
            scratch_shapes=[pltpu.VMEM((rows, width), LOW)],
        ),
        compiler_params=pltpu.CompilerParams(
            dimension_semantics=("arbitrary",), vmem_limit_bytes=56 << 20
        ),
        cost_estimate=BRIEF,
    )(place, *[mixed[p] for p in range(ranks)], out_full, tokens, gain[None])


def out_back_kernel(near, place, own_ref, *refs):
    near_refs = refs[:near]
    out_ref, state_ref, up_ref, gain_ref, *refs = refs[near:]
    grad_ref, attn_ref, kept_ref, sent_ref, gain_sum_ref, *back_refs = refs
    step = pl.program_id(0)

    @pl.when(step == 0)
    def _():
        grad = own_ref[...]
        for near_ref in near_refs:
            grad = grad + near_ref[...].astype(F32)
        state = state_ref[...]
        through, gain_sum = normed_back(state, inverse_rms(state), gain_ref[...], grad)
        grad = up_ref[...].astype(F32) + through
        grad_ref[...] = grad
        gain_sum_ref[...] = gain_sum[None]
        attn_ref[...] = (grad * live_rows(place, grad.shape[0])).astype(LOW)
        split_columns(place, attn_ref, kept_ref, sent_ref)

    back = rows_by(attn_ref[...], out_ref[...].reshape(-1, out_ref.shape[-1]), (1, 1)).astype(LOW)
    for k, back_ref in enumerate(back_refs):

        @pl.when(step == k)
        def _():
            back_ref[...] = back


def split_columns(place, source, kept, sent):
    size = lax.axis_size("dp")
    block = source.shape[1] // size
    for r in range(size):
        start = pl.multiple_of((place[2] ^ r) * block, block)
        target = sent if r % 2 else kept
        target[:, r // 2 * block : (r // 2 + 1) * block] = source[:, pl.ds(start, block)]


def out_back(own, near, out_full, state, cotangent, gain, place):
    rows, features = own.shape
    blocks, ranks, slice_rows, _ = out_full.shape
    width = blocks * slice_rows
    square, half = (rows, features), (rows, features // 2)
    shapes = [
        (square, F32), (square, LOW), (half, LOW), (half, LOW), ((1, features), F32),
        *[((rows, width), LOW)] * ranks,
    ]
    grad, _, kept, sent, gain_sum, *backs = pl.pallas_call(
        functools.partial(out_back_kernel, len(near)),
        name="out_back",
        out_shape=[jax.ShapeDtypeStruct(*shape) for shape in shapes],
        grid_spec=pltpu.PrefetchScalarGridSpec(
            num_scalar_prefetch=1,
            grid=(ranks,),
            in_specs=[whole(square)] * (1 + len(near))
            + [out_spec(out_full), whole(square), whole(square), whole((1, features))],
            out_specs=[whole(shape) for shape, _ in shapes],
        ),
        compiler_params=pltpu.CompilerParams(
            dimension_semantics=("arbitrary",), vmem_limit_bytes=56 << 20
        ),
        cost_estimate=BRIEF,
    )(place, own, *near, out_full, state, cotangent, gain[None])
    return grad, kept, sent, gain_sum[0], backs


def feed_kernel(
    place,
    rows_ref,
    branch_ref,
    gate_ref,
    up_ref,
    down_ref,
    made_ref,
    kept_ref,
    sent_ref,
    two_ref,
    mlp_ref,
    two_sum,
    mlp_sum,
):
    step = pl.program_id(0)

    @pl.when(step == 0)
    def _():
        two_sum[...] = jnp.zeros_like(two_sum)
        mlp_sum[...] = jnp.zeros_like(mlp_sum)
        for k, source in enumerate((rows_ref, branch_ref)):
            split_columns(place, source, kept_ref.at[k], sent_ref.at[k])

    rows = rows_ref[...]
    gate_pre = rows_by(rows, gate_ref[...], (1, 0))
    up_pre = rows_by(rows, up_ref[...], (1, 0))
    grad_hidden = rows_by(branch_ref[...], down_ref[...], (1, 1))
    scale, cube = 0.7978845608028654, 0.044715
    square = gate_pre * gate_pre
    bend = jnp.tanh(scale * (gate_pre + cube * (square * gate_pre)))
    half = 0.5 * (1.0 + bend)
    curved = gate_pre * half
    slope = half + (0.5 * scale) * gate_pre * (1.0 - bend * bend) * (1.0 + (3.0 * cube) * square)
    hidden = (curved * up_pre).astype(LOW)
    gate_back = (grad_hidden * up_pre * slope).astype(LOW)
    up_back = (grad_hidden * curved).astype(LOW)
    made_ref[0] = hidden
    made_ref[1] = gate_back
    made_ref[2] = up_back
    two_sum[...] += rows_by(gate_back, gate_ref[...], (1, 1)) + rows_by(up_back, up_ref[...], (1, 1))
    mlp_sum[...] += rows_by(hidden, down_ref[...], (1, 0))

    @pl.when(step == pl.num_programs(0) - 1)
    def _():
        two_ref[...] = two_sum[...].astype(two_ref.dtype)
        mlp_ref[...] = mlp_sum[...].astype(mlp_ref.dtype)


def feed_forward(rows, branch, gate_weight, up_weight, down_weight, place, kind):
    count, features = rows.shape
    units = gate_weight.shape[1]
    tile = min(512, units)
    columns = pl.BlockSpec((features, tile), lambda step, place: (0, step))
    half = (2, count, features // 2)
    return pl.pallas_call(
        feed_kernel,
        name="feed_forward",
        out_shape=(
            jax.ShapeDtypeStruct((3, count, units), LOW),
            *[jax.ShapeDtypeStruct(half, LOW)] * 2,
            *[jax.ShapeDtypeStruct((count, features), kind)] * 2,
        ),
        grid_spec=pltpu.PrefetchScalarGridSpec(
            num_scalar_prefetch=1,
            grid=(units // tile,),
            in_specs=[
                whole((count, features)),
                whole((count, features)),
                columns,
                columns,
                pl.BlockSpec((tile, features), lambda step, place: (step, 0)),
            ],
            out_specs=[
                pl.BlockSpec((3, count, tile), lambda step, place: (0, 0, step)),
                *[whole(half)] * 2,
                *[whole((count, features))] * 2,
            ],
            scratch_shapes=[pltpu.VMEM((count, features), F32)] * 2,
        ),
        compiler_params=pltpu.CompilerParams(
            dimension_semantics=("arbitrary",), vmem_limit_bytes=44 << 20
        ),
        cost_estimate=BRIEF,
    )(place, rows, branch, gate_weight, up_weight, down_weight)


def project_back_kernel(*refs):
    count = (len(refs) - 2) // 3
    rows_refs, one_refs, weight_ref = refs[:count], refs[count : 2 * count], refs[2 * count]
    out_refs, gain_ref = refs[2 * count + 1 : -1], refs[-1]
    weight = weight_ref[...]
    gain = jnp.zeros(gain_ref.shape, F32)
    for rows_ref, one_ref, out_ref in zip(rows_refs, one_refs, out_refs):
        value = rows_by(rows_ref[...], weight, (1, 1))
        out_ref[...] = value.astype(out_ref.dtype)
        gain = gain + jnp.sum(value * one_ref[...].astype(F32), axis=0, keepdims=True)
    gain_ref[...] = gain


def project_rows_back(rows, weight, count, one, wanted, kinds):
    features, wide = weight.shape
    tile = min(512, features)
    made = pl.BlockSpec((count, tile), lambda step: (0, step))
    *parts, gain = pl.pallas_call(
        project_back_kernel,
        name="project_back",
        out_shape=[jax.ShapeDtypeStruct((count, features), kind) for kind in kinds]
        + [jax.ShapeDtypeStruct((1, features), F32)],
        grid=(features // tile,),
        in_specs=[pl.BlockSpec((count, wide), lambda step, p=p: (p, 0)) for p in wanted]
        + [made] * len(wanted)
        + [pl.BlockSpec((tile, wide), lambda step: (step, 0))],
        out_specs=[made] * len(wanted) + [pl.BlockSpec((1, tile), lambda step: (0, step))],
        compiler_params=pltpu.CompilerParams(
            dimension_semantics=("arbitrary",), vmem_limit_bytes=56 << 20
        ),
        cost_estimate=BRIEF,
    )(*[rows] * len(wanted), *[one[p] for p in wanted], weight)
    return dict(zip(wanted, parts)), gain[0]


def weight_kernel(*refs):
    *in_refs, low_keep, low_send, high_keep, high_send = refs
    half = len(in_refs) // 2
    step = pl.program_id(0)
    steps = pl.num_programs(0)
    value = rows_by(in_refs[0][...], in_refs[half][...], (0, 0))
    for left, right in zip(in_refs[1:half], in_refs[half + 1 :]):
        value = value + rows_by(left[...], right[...], (0, 0))
    value = value.astype(LOW)
    middle = value.shape[0] // 2
    odd = lax.rem(step, 2) == 1
    upper = step >= steps // 2

    @pl.when(jnp.logical_not(odd))
    def _():
        low_keep[...] = value[:middle]

    @pl.when(odd)
    def _():
        low_send[...] = value[:middle]

    @pl.when(jnp.logical_not(upper))
    def _():
        high_keep[...] = value[middle:]

    @pl.when(upper)
    def _():
        high_send[...] = value[middle:]


def weight_blocks(lefts, rights, blocks):
    across = lefts[0][0].shape[2] // blocks
    along = rights[0][0].shape[2]

    def left_spec(pair):
        return pl.BlockSpec((None, pair[0].shape[1], across), lambda step: (pair[1], 0, step))

    def right_spec(pair):
        return pl.BlockSpec((None, pair[0].shape[1], along), lambda step: (pair[1], 0, 0))

    def out_spec_of(place):
        return pl.BlockSpec((None, across // 2, along), lambda step: (place(step), 0, 0))

    half = blocks // 2
    return pl.pallas_call(
        weight_kernel,
        name="weight_blocks",
        out_shape=[jax.ShapeDtypeStruct((half, across // 2, along), LOW)] * 4,
        grid=(blocks,),
        in_specs=[left_spec(pair) for pair in lefts] + [right_spec(pair) for pair in rights],
        out_specs=[
            out_spec_of(lambda step: lax.div(step, 2)),
            out_spec_of(lambda step: lax.div(step, 2)),
            out_spec_of(lambda step: jnp.minimum(step, half - 1)),
            out_spec_of(lambda step: jnp.maximum(step - half, 0)),
        ],
        compiler_params=pltpu.CompilerParams(
            dimension_semantics=("arbitrary",), vmem_limit_bytes=40 << 20
        ),
        cost_estimate=BRIEF,
    )(*[pair[0] for pair in lefts], *[pair[0] for pair in rights])


def inverse_rms(values):
    return lax.rsqrt(jnp.mean(values * values, axis=-1, keepdims=True) + EPS)


def normed_back(values, inverse, gain_vec, grad):
    unit = values * inverse
    scaled = grad * gain_vec
    grad_values = inverse * (scaled - unit * jnp.mean(scaled * unit, axis=-1, keepdims=True))
    return grad_values, jnp.sum(grad * unit, axis=0)


def hold(value):
    return lax.optimization_barrier(value)


def shards(
    tokens,
    cotangent,
    lengths,
    query_weight,
    key_weight,
    value_weight,
    out_weight,
    gate_weight,
    up_weight,
    down_weight,
    attn_gain,
    mlp_gain,
    memory_gate,
):
    ranks = lax.axis_size("mp")
    row_count = tokens.shape[0]
    width = query_weight.shape[1]
    heads = width // DK
    per_chunk = row_count // SEG
    rank = lax.axis_index("mp")
    pieces = range(ranks)
    place = jnp.stack([rank, lengths[0], lax.axis_index("dp")]).astype(jnp.int32)
    live = (rank * row_count + jnp.arange(row_count) < lengths[0]).astype(F32)[:, None]
    share = jax.nn.sigmoid(memory_gate)

    features = tokens.shape[1]
    blocks = lax.axis_size("dp")
    near, far = singles(ranks), doubles(ranks)

    def product(left, right):
        return rows_by(left, right, (0, 0)).astype(LOW)

    inputs = tokens.astype(F32)
    inverse_one = inverse_rms(inputs)
    normed_one = (inputs * inverse_one * attn_gain).astype(LOW)
    slice_rows = width // blocks
    out_slice = lax.dynamic_slice_in_dim(
        out_weight, lax.axis_index("dp") * slice_rows, slice_rows, axis=0
    )
    out_slice, normed_one = hold((out_slice, normed_one))
    qkv_weight = jnp.concatenate([query_weight, key_weight, value_weight], axis=1)

    def project(rows):
        return rows_by(rows, qkv_weight, (1, 0)).astype(LOW)

    one = gather_near(normed_one, "mp")
    out_slices = gather_near(out_slice, "mp")
    qkv = {0: project(one[0])}
    one, out_slices, qkv, qkv_weight = hold((one, out_slices, qkv, qkv_weight))

    one.update(gather_far(one, "mp"))
    out_slices.update(gather_far(out_slices, "mp"))
    qkv.update({p: project(one[p]) for p in near})
    upstream = cotangent.astype(F32)
    branch_mine = (upstream * live).astype(LOW)
    one, out_slices, qkv, branch_mine = hold((one, out_slices, qkv, branch_mine))
    out_full = lax.all_gather(
        jnp.stack([out_slices[p] for p in pieces]), "dp", axis=0, tiled=True
    )

    branch = gather_near(branch_mine, "mp")
    qkv.update({p: project(one[p]) for p in far})
    qkv = stacked(qkv)
    mixed, memories, normers = attend(qkv, place, share, per_chunk)
    mixed = hold(mixed)

    mixed = swap_pieces(
        {p: mixed[p * row_count : (p + 1) * row_count] for p in pieces}, "mp"
    )
    mixed, branch = hold((mixed, branch))

    out_full = out_full.reshape(blocks, ranks, slice_rows, features)
    state, normed_two, mixed = out_project(mixed, out_full, tokens, mlp_gain, place)

    made, kept, sent, two_parts, mlp_parts = {}, {}, {}, {}, {}

    def feed(p):
        kind = LOW if p == 1 or p in far else F32
        made[p], kept[p], sent[p], two_parts[p], mlp_parts[p] = feed_forward(
            two[p], branch[p], gate_weight, up_weight, down_weight, place, kind
        )

    their_made, their_kept = {}, {}

    def share_rows(p):
        their_made[p] = hop(made[p], "dp", 1)
        their_kept[p] = hop(sent[p], "dp", 1)

    two = gather_near(normed_two, "mp")
    branch.update(gather_far(branch, "mp"))
    feed(0)
    one_kept, one_sent = relative_blocks(stacked(one), "dp")
    their_mixed = hop(mixed, "dp", 1)
    two, made, kept, sent, two_parts, mlp_parts, branch, one_kept, one_sent, their_mixed = hold(
        (two, made, kept, sent, two_parts, mlp_parts, branch, one_kept, one_sent, their_mixed)
    )

    two.update(gather_far(two, "mp"))
    share_rows(0)
    their_one = hop(one_sent, "dp", 1)
    feed(1)
    two, made, kept, sent, two_parts, mlp_parts, their_made, their_kept, their_one = hold(
        (two, made, kept, sent, two_parts, mlp_parts, their_made, their_kept, their_one)
    )

    mlp_near = reduce_near(mlp_parts, None, "mp", (1,))
    share_rows(1)
    for p in far:
        feed(p)
    two, made, kept, sent, two_parts, mlp_parts, their_made, their_kept, mlp_near = hold(
        (two, made, kept, sent, two_parts, mlp_parts, their_made, their_kept, mlp_near)
    )

    two_far = reduce_far(two_parts, "mp")
    for p in far:
        share_rows(p)
    for p in near[1:]:
        feed(p)
    made, kept, sent, two_parts, mlp_parts, their_made, their_kept, two_far = hold(
        (made, kept, sent, two_parts, mlp_parts, their_made, their_kept, two_far)
    )

    steps = device_steps("dp")

    def weights_of(left, right):
        return DeviceSum(
            weight_blocks(
                [(kept[p], left) for p in pieces] + [(their_kept[p], left) for p in pieces],
                [(made[p], right) for p in pieces] + [(their_made[p], right) for p in pieces],
                blocks // 2,
            ),
            "dp",
        )

    two_near = reduce_near(two_parts, two_far, "mp")
    for p in near[1:]:
        share_rows(p)
    gate_sum = weights_of(0, 1)
    fly(gate_sum)
    up_sum = weights_of(0, 2)
    down_sum = weights_of(1, 0)
    two_near, mlp_parts, gate_sum.state, up_sum.state, down_sum.state = hold(
        (two_near, mlp_parts, gate_sum.state, up_sum.state, down_sum.state)
    )

    mlp_far = reduce_far(mlp_parts, "mp")
    fly(up_sum)
    grad_state, attn_kept, attn_sent, grad_mlp_gain, grad_mixed = out_back(
        two_parts[0],
        [two_near[p] for p in sorted(two_near)],
        out_full,
        state,
        cotangent,
        mlp_gain,
        place,
    )
    their_attn = hop(attn_sent, "dp", 1)
    (
        mlp_far, grad_mixed, attn_kept, their_attn, grad_state, grad_mlp_gain, mlp_parts,
        gate_sum.state, up_sum.state, down_sum.state,
    ) = hold(
        (
            mlp_far, grad_mixed, attn_kept, their_attn, grad_state, grad_mlp_gain, mlp_parts,
            gate_sum.state, up_sum.state, down_sum.state,
        )
    )
    grad_mixed = swap_pieces(grad_mixed, "mp")
    fly(down_sum)
    out_sum = DeviceSum(
        weight_blocks(
            [(attn_kept[None], 0), (their_attn[None], 0)],
            [(mixed[None], 0), (their_mixed[None], 0)],
            blocks // 2,
        ),
        "dp",
    )
    gate_sum.land()
    up_sum.land()
    grad_mixed, mlp_parts, gate_sum.state, up_sum.state, down_sum.state, out_sum.state = hold(
        (grad_mixed, mlp_parts, gate_sum.state, up_sum.state, down_sum.state, out_sum.state)
    )

    mlp_near.update(reduce_near(mlp_parts, mlp_far, "mp", near[1:]))
    fly(out_sum, *([gate_sum, up_sum] if steps > 1 else []))
    down_sum.land()
    grad_qkv, grad_mix = attend_back(
        qkv, [grad_mixed[p] for p in pieces], memories, normers, place, share, per_chunk
    )
    grad_qkv, grad_mix, mlp_near, out_sum.state, down_sum.state, gate_sum.state, up_sum.state = hold(
        (grad_qkv, grad_mix, mlp_near, out_sum.state, down_sum.state, gate_sum.state, up_sum.state)
    )

    def project_back(wanted):
        kinds = [LOW if p == 1 or p in far else F32 for p in wanted]
        return project_rows_back(grad_qkv, qkv_weight, row_count, one, wanted, kinds)

    their_qkv = hop(grad_qkv, "dp", 1)
    one_parts, gain_far = project_back(far)
    one_parts, grad_qkv, out_sum.state, down_sum.state, mlp_near = hold(
        (one_parts, grad_qkv, out_sum.state, down_sum.state, mlp_near)
    )
    one_far = reduce_far(one_parts, "mp")
    qkv_sum = DeviceSum(
        weight_blocks(
            [(one_kept[None], 0), (their_one[None], 0)],
            [(grad_qkv[None], 0), (their_qkv[None], 0)],
            blocks // 2,
        ),
        "dp",
    )
    grad_qkv, qkv_sum.state, out_sum.state, down_sum.state = hold(
        (grad_qkv, qkv_sum.state, out_sum.state, down_sum.state)
    )
    out_sum.land()
    if steps > 1:
        fly(down_sum, out_sum)
    more_parts, gain_near = project_back([0] + near)
    one_parts.update(more_parts)
    one_parts, one_far, qkv_sum.state, mlp_near = hold(
        (one_parts, one_far, qkv_sum.state, mlp_near)
    )

    one_near = reduce_near(one_parts, one_far, "mp")
    block_out = (state + live * total(mlp_parts[0], mlp_near)).astype(LOW)
    grad_attn_gain = (gain_far + gain_near) / attn_gain
    grad_share = jnp.sum(grad_mix, axis=1) * share * (1.0 - share)
    share_full = lax.dynamic_update_slice(
        jnp.zeros((heads * ranks,), F32), grad_share, (rank * heads,)
    )
    small = jnp.concatenate([grad_attn_gain, grad_mlp_gain, share_full])
    fly(qkv_sum)
    for k in range(1, steps):
        for some in ([gate_sum, up_sum], [down_sum, out_sum]):
            for one_sum in some:
                one_sum.land()
            if k + 1 < steps:
                fly(*some)
        qkv_sum.land()
        fly(qkv_sum)
    qkv_sum.land()
    grad_gate, grad_up = gate_sum.result(), up_sum.result()
    grad_down = down_sum.result().T
    grad_proj = qkv_sum.result()
    grad_out_part = out_sum.result()
    out_parts = {p: grad_out_part[:, p * width : (p + 1) * width] for p in pieces}
    out_parts = {p: out_parts[p].astype(LOW) if p else out_parts[p] for p in pieces}
    one_near, small, out_parts, block_out, grad_gate, grad_up, grad_down, grad_proj = hold(
        (one_near, small, out_parts, block_out, grad_gate, grad_up, grad_down, grad_proj)
    )

    small = sum_everywhere(sum_everywhere(small, "mp"), "dp")
    grad_out = total(
        out_parts[0], {p: hop(out_parts[p], "mp", p) for p in range(1, ranks)}
    ).T
    grad_query, grad_key, grad_value = (
        grad_proj[:, j * width : (j + 1) * width] for j in range(3)
    )
    grad_normed_one = total(one_parts[0], one_near)
    grad_inputs = normed_back(inputs, inverse_one, attn_gain, grad_normed_one)[0]
    grad_tokens = grad_state + grad_inputs
    return (
        block_out,
        grad_tokens,
        grad_query,
        grad_key,
        grad_value,
        grad_out,
        grad_gate,
        grad_up,
        grad_down,
        small[:features],
        small[features : 2 * features],
        small[2 * features : 2 * features + heads * ranks],
    )


def solution(mesh):
    return jax.shard_map(
        shards,
        mesh=mesh,
        in_specs=(
            P(("dp", "mp"), None),
            P(("dp", "mp"), None),
            P("dp"),
            P(None, "mp"),
            P(None, "mp"),
            P(None, "mp"),
            P("mp", None),
            P(None, "mp"),
            P(None, "mp"),
            P("mp", None),
            P(),
            P(),
            P("mp"),
        ),
        out_specs=(
            P(("dp", "mp"), None),
            P(("dp", "mp"), None),
            P("dp", "mp"),
            P("dp", "mp"),
            P("dp", "mp"),
            P("mp", "dp"),
            P("dp", "mp"),
            P("dp", "mp"),
            P("mp", "dp"),
            P(),
            P(),
            P(),
        ),
        check_vma=False,
    )
```
